32 devices in a mesh: row: 4 (over y, x), col: 8 (over z, core).
Axes of the slice: x: 2, y: 2, z: 4, core: 2. Of those that a mesh axis runs over, the one named last changes fastest.
Arguments:
- inverse: bfloat16 [26624, 26624], P('row', 'col'), may hold values from -6 to 6
- panels: bfloat16 [2, 8192, 512], P(None, 'col'), may hold values from -0.0625 to 0.0625
- block_slot: int32 [208], replicated, may hold values from 0 to 207, as said below
- list_ids: int32 [2, 64], replicated, may hold values from 0 to 207, as said below
Outputs:
- packed_panels: float32 [2, 16384, 512], P(None, ('row', 'col'))
- diag_update: float32 [2, 512, 512], replicated
The draws below stay inside these ranges and needn't reach their ends.
Inputs may be any that keep to these rules, and one draw needn't show every extreme that they name: block_slot is a permutation of the slots. `list_ids`: each supernode lists distinct blocks; at most 32 of a supernode's listed blocks have slots in one grid row (slot // 52 equal), and in every supernode some grid row holds exactly 32. `list_ids`: in each aligned group of 8 list positions of a supernode, at most 4 listed blocks have slots in one grid column (slot // 26 equal).
All inputs are finite; a program needn't handle non-finite values.
Results may differ from the reference program's by a relative error of at most 0.0003.
Values may be sent and summed in bfloat16 or wider, within the bound.
No kernel may reach another device: no remote copies, remote signals or barrier semaphores. Data moves between devices by JAX's collectives and lax.ppermute only.
A program may use at most 192 MiB of HBM per device.

```python
import jax
import jax.numpy as jnp
from jax import lax

ORDER = 26624
BS = 128
W = 512
SUPER = 2
LIST = 64
NBLK = 208
RB = 52
CB = 26
MAXR = 32
N_ROW = 4
N_COL = 8


def make_lists(key):
    perm = jax.random.permutation(jax.random.fold_in(key, 11), NBLK).astype(jnp.int32)
    inverse_perm = jnp.argsort(perm).astype(jnp.int32)
    grid_rows = NBLK // RB
    spare = LIST - MAXR
    base_count = spare // (grid_rows - 1)
    extra_count = spare % (grid_rows - 1)
    ranks = jnp.arange(grid_rows, dtype=jnp.int32)
    by_rank = jnp.where(ranks == 0, MAXR, base_count + jnp.where(ranks - 1 < extra_count, 1, 0)).astype(jnp.int32)
    lists = []
    for supernode in range(SUPER):
        super_key = jax.random.fold_in(key, 100 + supernode)
        row_perm = jax.random.permutation(jax.random.fold_in(super_key, 1), grid_rows)
        counts = jnp.zeros((grid_rows,), jnp.int32).at[row_perm].set(by_rank)
        row_keys = jax.random.split(jax.random.fold_in(super_key, 2), grid_rows)
        local_perm = jax.vmap(lambda one_key: jax.random.permutation(one_key, RB))(row_keys).astype(jnp.int32)
        within = jnp.arange(RB, dtype=jnp.int32)[None, :] < counts[:, None]
        slot_grid = jnp.arange(grid_rows, dtype=jnp.int32)[:, None] * RB + local_perm
        scores = jax.random.permutation(jax.random.fold_in(super_key, 3), grid_rows * RB).astype(jnp.int32)
        keyed = jnp.where(within.reshape(-1), scores, grid_rows * RB + scores)
        picked = jnp.argsort(keyed, stable=True)[:LIST]
        chosen_slots = slot_grid.reshape(-1)[picked].astype(jnp.int32)
        col_of = (chosen_slots // CB).astype(jnp.int32)
        order_scores = jax.random.permutation(jax.random.fold_in(super_key, 4), LIST).astype(jnp.int32)
        ordered = chosen_slots[jnp.argsort(col_of * LIST + order_scores, stable=True)]
        first_col = (ordered[0] // CB).astype(jnp.int32)
        grid_cols = NBLK // CB
        shift_by = (first_col + grid_cols // 2) % grid_cols
        index = jnp.arange(LIST, dtype=jnp.int32)
        target = (index + shift_by) % N_COL * (LIST // N_COL) + index // N_COL
        placed = jnp.zeros((LIST,), jnp.int32).at[target].set(ordered)
        lists.append(inverse_perm[placed])
    return (perm, jnp.stack(lists).astype(jnp.int32))


def draw_block_slot(key, part):
    return make_lists(key)[0]


def draw_list_ids(key, part):
    return make_lists(key)[1]


def shard_levels(rng, shape, cuts, least, high):
    level = 1.0
    for position, blocks in cuts:
        steps = jax.random.uniform(jax.random.fold_in(jax.random.fold_in(rng, 6), position), (blocks,), jnp.float32, least / len(cuts), high / len(cuts))
        level = level * jnp.repeat(jnp.exp(steps), shape[position] // blocks).reshape((-1,) + (1,) * (len(shape) - 1 - position))
    return level


def gaussian(own_key, shape, spread, bound, cuts=(), held_as=jnp.bfloat16):
    result = spread * jax.random.normal(own_key, shape, jnp.float32)
    if cuts:
        result = result * shard_levels(own_key, shape, cuts, -0.22, 0.18)
    return jnp.clip(result, -bound, bound).astype(held_as)


def setup_inputs(seed: int = 0) -> dict:
    key_of = jax.random.split(jax.random.key(seed), 5)
    return {
        "inverse": gaussian(key_of[0], (ORDER, ORDER), 1.0, 6.0, ((0, 4), (1, 8))),
        "panels": gaussian(key_of[1], (SUPER, LIST * BS, W), (LIST * BS) ** -0.5, 0.0625, ((1, 8),)),
        "block_slot": draw_block_slot(jax.random.fold_in(key_of[4], 71), 0),
        "list_ids": draw_list_ids(jax.random.fold_in(key_of[4], 71), 0),
    }


def reference(inverse, panels, block_slot, list_ids):
    blocked = inverse.reshape(NBLK, BS, NBLK, BS)
    packed_all = []
    diag_all = []
    positions = jnp.arange(LIST, dtype=jnp.int32)
    for supernode in range(SUPER):
        slots = block_slot[list_ids[supernode]].astype(jnp.int32)
        picked = blocked[slots[:, None], :, slots[None, :], :]
        picked = jnp.transpose(picked, (0, 2, 1, 3)).reshape(LIST * BS, LIST * BS)
        sums = jnp.dot(picked, panels[supernode], preferred_element_type=jnp.float32)
        diag_terms = -jnp.dot(panels[supernode].astype(jnp.float32).T, sums, precision=lax.Precision.HIGHEST)
        grid_row = (slots // RB).astype(jnp.int32)
        sum_blocks = sums.reshape(LIST, BS, W)

        def pack_row(row_id):
            keyed = jnp.where(grid_row == row_id, positions, LIST + positions)
            chosen = jnp.argsort(keyed, stable=True)[:MAXR]
            is_valid = grid_row[chosen] == row_id
            return jnp.where(is_valid[:, None, None], sum_blocks[chosen], jnp.zeros((), jnp.float32))

        packed = jax.vmap(pack_row)(jnp.arange(N_ROW, dtype=jnp.int32)).reshape(N_ROW * MAXR * BS, W)
        packed_all.append(packed)
        diag_all.append(diag_terms)
    return jnp.stack(packed_all), jnp.stack(diag_all)
```

```python
import functools

import jax
import jax.numpy as jnp
from jax import lax
from jax.experimental import pallas as pl
from jax.experimental.pallas import tpu as pltpu
from jax.sharding import PartitionSpec as P

BS = 128
GROUP = 4
TAIL = 16
AXES = ("row", "col")


def swap_bit(bits, parity, bit):
    return 1 << (bit if parity == 0 else bits - 1 - bit)


def row_swap(n_row, n_col, bit):
    bits = n_row.bit_length() - 1
    return [
        ((r ^ swap_bit(bits, c % 2, bit)) * n_col + c, r * n_col + c)
        for r in range(n_row)
        for c in range(n_col)
    ]


def core_swap(n_col):
    return [(c ^ 1, c) for c in range(n_col)]


def line_shift(n_col, shift):
    return [((c + 2 * shift) % n_col, c) for c in range(n_col)]


def pick_table(hit, value, capacity):
    listed = hit.shape[1]
    pos = jnp.arange(listed, dtype=jnp.int32)
    ahead = (pos[:, None] < pos[None, :]) & hit[:, :, None]
    rank = jnp.sum(ahead.astype(jnp.int32), axis=1)
    here = hit[:, None, :] & (rank[:, None, :] == jnp.arange(capacity, dtype=jnp.int32)[None, :, None])
    both = jnp.stack([jnp.broadcast_to(pos, hit.shape), value], axis=1)
    return jnp.sum(jnp.where(here[:, None], both[:, :, None, :], 0), axis=-1)


def encode(rows):
    top = jnp.max(jnp.abs(rows), axis=0, keepdims=True)
    exponent = jnp.ceil(jnp.log2(jnp.maximum(top, 2.0**-100)))
    scaled = rows * jnp.exp2(15.0 - exponent)
    rounded = scaled + jnp.where(scaled >= 0, 0.5, -0.5)
    rounded = jnp.clip(rounded, -32767.0, 32767.0)
    tail = jnp.broadcast_to(exponent, (TAIL, rows.shape[1]))
    return rounded.astype(jnp.int32).astype(jnp.int16), tail.astype(jnp.int32).astype(jnp.int16)


def decode(coded, tail):
    scale = jnp.exp2(tail[0:1].astype(jnp.int32).astype(jnp.float32) - 15.0)
    return coded.astype(jnp.int32).astype(jnp.float32) * scale


def product_kernel(dims, tab, inverse, *refs):
    n_row, n_col, per_col, max_rows, max_cols, sub = dims
    bits = n_row.bit_length() - 1
    n_line = n_col // 2
    in_chunk = max_rows // n_col
    own = refs[0:2]
    pieces = (refs[2 : 2 + n_row], refs[2 + n_row : 2 + 2 * n_row])
    coded, plain, diag, cols_buf, rows_buf, strips, acc, cols_sem, rows_sem, strip_sem = refs[2 + 2 * n_row :]
    step = pl.program_id(0)
    chunk_rows = in_chunk * BS
    group_rows = GROUP * BS
    base = 2 * max_rows + 2 * max_cols
    n_rows, n_cols, my_row, my_col = tab[base], tab[base + 1], tab[base + 2], tab[base + 3]
    my_parity = lax.rem(my_col, 2)
    my_z = lax.div(my_col, 2)

    def chunk_of(at):
        shift = lax.rem(at, n_line)
        parity = jnp.where(at < n_line, 1 - my_parity, my_parity)
        return 2 * lax.rem(my_z + shift, n_line) + parity

    def fetch(listed, buf, at, sem):
        source = lax.div(listed, per_col)
        item = lax.rem(listed, per_col)
        parity = lax.rem(source, 2)
        swapped = parity != my_parity
        shift = lax.rem(lax.div(source, 2) - my_z + n_line, n_line)
        start = pl.multiple_of(at * BS, BS)
        for other in (0, 1):
            mine = swapped if other else jnp.logical_not(swapped)

            @pl.when(mine & (shift == 0))
            def _(other=other):
                pltpu.make_async_copy(own[other].at[item], buf.at[pl.ds(start, BS)], sem).start()

            @pl.when(mine & (shift != 0))
            def _(other=other):
                for e in range(n_row):
                    masks = [sum(swap_bit(bits, p, b) for b in range(bits) if e >> b & 1) for p in (0, 1)]
                    mask = jnp.where(parity == 0, masks[0], masks[1])
                    place = pl.multiple_of(start + (my_row ^ mask) * sub, sub)
                    pltpu.make_async_copy(
                        pieces[other][e].at[(shift - 1) * per_col + item], buf.at[pl.ds(place, sub)], sem
                    ).start()

    def strip_copy(chunk, item, slot):
        block = tab[max_rows + chunk * in_chunk + item]
        return pltpu.make_async_copy(
            inverse.at[pl.ds(pl.multiple_of(block * BS, BS), BS)],
            strips.at[slot, pl.ds(item * BS, BS)],
            strip_sem.at[slot, item],
        )

    def start_strips(chunk, slot):
        @pl.when(chunk * in_chunk < n_rows)
        def _():
            for item in range(in_chunk):
                strip_copy(chunk, item, slot).start()

    slot = lax.rem(step, 2)
    chunk = chunk_of(step)

    @pl.when(step == 0)
    def _():
        start_strips(chunk, 0)

        @pl.loop(0, n_cols)
        def _(j):
            fetch(tab[2 * max_rows + j], cols_buf, j, cols_sem.at[j])

        @pl.loop(0, n_rows)
        def _(k):
            fetch(tab[k], rows_buf, k, rows_sem.at[k])

        @pl.loop(n_cols, lax.div(n_cols + GROUP - 1, GROUP) * GROUP)
        def _(j):
            cols_buf[pl.ds(pl.multiple_of(j * BS, BS), BS), :] = jnp.zeros((BS, cols_buf.shape[1]), cols_buf.dtype)

        @pl.loop(n_rows, lax.div(n_rows + in_chunk - 1, in_chunk) * in_chunk)
        def _(k):
            rows_buf[pl.ds(pl.multiple_of(k * BS, BS), BS), :] = jnp.zeros((BS, rows_buf.shape[1]), rows_buf.dtype)

        diag[...] = jnp.zeros_like(diag)

        @pl.loop(0, n_cols)
        def _(j):
            part = cols_buf.at[pl.ds(pl.multiple_of(j * BS, BS), BS)]
            pltpu.make_async_copy(part, part, cols_sem.at[j]).wait()

        @pl.loop(0, n_rows)
        def _(k):
            part = rows_buf.at[pl.ds(pl.multiple_of(k * BS, BS), BS)]
            pltpu.make_async_copy(part, part, rows_sem.at[k]).wait()

    @pl.when(step + 1 < 2 * n_line)
    def _():
        start_strips(chunk_of(step + 1), 1 - slot)

    left = n_rows - chunk * in_chunk
    acc[...] = jnp.zeros_like(acc)

    @pl.when(left > 0)
    def _():
        for item in range(in_chunk):
            strip_copy(chunk, item, slot).wait()

        @pl.loop(0, lax.div(n_cols + GROUP - 1, GROUP))
        def _(k):
            parts = []
            for item in range(GROUP):
                col = tab[2 * max_rows + max_cols + k * GROUP + item]
                parts.append(strips[slot, :, pl.ds(pl.multiple_of(col * BS, BS), BS)])
            right = cols_buf[pl.ds(pl.multiple_of(k * group_rows, group_rows), group_rows), :]
            acc[...] += jnp.dot(jnp.concatenate(parts, axis=1), right, preferred_element_type=jnp.float32)

        row_ids = lax.broadcasted_iota(jnp.int32, acc.shape, 0)
        sums = jnp.where(row_ids < left * BS, acc[...], 0.0)
        acc[...] = sums
        high = sums.astype(jnp.bfloat16)
        low = (sums - high.astype(jnp.float32)).astype(jnp.bfloat16)
        rows = rows_buf[pl.ds(pl.multiple_of(chunk * chunk_rows, chunk_rows), chunk_rows), :]
        dims_t = (((0,), (0,)), ((), ()))
        diag[...] += lax.dot_general(rows, high, dims_t, preferred_element_type=jnp.float32)
        diag[...] += lax.dot_general(rows, low, dims_t, preferred_element_type=jnp.float32)

    @pl.when(step < n_line)
    def _():
        body, tail = encode(acc[...])
        coded[0, 0:chunk_rows, :] = body
        coded[0, chunk_rows:, :] = tail

    @pl.when(step >= n_line)
    def _():
        plain[0] = acc[...]


def products(tab, inverse, own, pieces, dims):
    n_row, n_col, per_col, max_rows, max_cols, sub = dims
    n_line = n_col // 2
    width = own[0].shape[-1]
    in_chunk = max_rows // n_col
    chunk_rows = in_chunk * BS
    any_spec = pl.BlockSpec(memory_space=pl.ANY)
    operands = [inverse, *own, *pieces[0], *pieces[1]]
    return pl.pallas_call(
        functools.partial(product_kernel, dims),
        out_shape=(
            jax.ShapeDtypeStruct((n_line, chunk_rows + TAIL, width), jnp.int16),
            jax.ShapeDtypeStruct((n_line, chunk_rows, width), jnp.float32),
            jax.ShapeDtypeStruct((width, width), jnp.float32),
        ),
        grid_spec=pltpu.PrefetchScalarGridSpec(
            num_scalar_prefetch=1,
            grid=(2 * n_line,),
            in_specs=[any_spec] * len(operands),
            out_specs=[
                pl.BlockSpec((1, chunk_rows + TAIL, width), lambda g, tab: (jnp.minimum(g, n_line - 1), 0, 0)),
                pl.BlockSpec((1, chunk_rows, width), lambda g, tab: (jnp.maximum(g - n_line, 0), 0, 0)),
                pl.BlockSpec((width, width), lambda g, tab: (0, 0)),
            ],
            scratch_shapes=[
                pltpu.VMEM((max_cols * BS, width), jnp.bfloat16),
                pltpu.VMEM((max_rows * BS, width), jnp.bfloat16),
                pltpu.VMEM((2, chunk_rows, inverse.shape[1]), jnp.bfloat16),
                pltpu.VMEM((chunk_rows, width), jnp.float32),
                pltpu.SemaphoreType.DMA((max_cols,)),
                pltpu.SemaphoreType.DMA((max_rows,)),
                pltpu.SemaphoreType.DMA((2, in_chunk)),
            ],
        ),
        compiler_params=pltpu.CompilerParams(dimension_semantics=("arbitrary",)),
        cost_estimate=pl.CostEstimate(flops=10**10, bytes_accessed=3 * 10**7, transcendentals=0),
        name="products",
    )(tab, *operands)


def pair_kernel(plain_ref, coded_ref, first_ref, *outs):
    chunk_rows = plain_ref.shape[1]
    step = pl.program_id(0)
    total = plain_ref[0] + decode(coded_ref[0, 0:chunk_rows, :], coded_ref[0, chunk_rows:, :])

    @pl.when(step == 0)
    def _():
        first_ref[...] = total

    for shift, out in enumerate(outs, 1):

        @pl.when(step == shift)
        def _(out=out):
            body, tail = encode(total)
            out[0:chunk_rows, :] = body
            out[chunk_rows:, :] = tail


def pair_sums(plain, coded):
    n_line, chunk_rows, width = plain.shape
    coded_shape = (chunk_rows + TAIL, width)
    whole = lambda shape: pl.BlockSpec(shape, lambda g: (0, 0))
    return pl.pallas_call(
        pair_kernel,
        out_shape=(jax.ShapeDtypeStruct((chunk_rows, width), jnp.float32),)
        + (jax.ShapeDtypeStruct(coded_shape, jnp.int16),) * (n_line - 1),
        grid=(n_line,),
        in_specs=[
            pl.BlockSpec((1, chunk_rows, width), lambda g: (g, 0, 0)),
            pl.BlockSpec((1, *coded_shape), lambda g: (g, 0, 0)),
        ],
        out_specs=[whole((chunk_rows, width))] + [whole(coded_shape)] * (n_line - 1),
        cost_estimate=pl.CostEstimate(flops=10**7, bytes_accessed=9 * 10**6, transcendentals=0),
        name="pair_sums",
    )(plain, coded)


def final_kernel(count, *refs):
    out = refs[-1]
    for supernode in range(out.shape[0]):
        first, *coded = refs[supernode * count : (supernode + 1) * count]
        total = first[...]
        for part in coded:
            total = total + decode(part[0 : total.shape[0], :], part[total.shape[0] :, :])
        out[supernode] = total


def final_sums(parts):
    chunk_rows, width = parts[0][0].shape
    operands = [array for one in parts for array in one]
    return pl.pallas_call(
        functools.partial(final_kernel, len(parts[0])),
        out_shape=jax.ShapeDtypeStruct((len(parts), chunk_rows, width), jnp.float32),
        cost_estimate=pl.CostEstimate(flops=10**7, bytes_accessed=7 * 10**6, transcendentals=0),
        name="final_sums",
    )(*operands)


def sum_over_all(terms, n_row, n_col, my_row, my_col):
    bits = n_row.bit_length() - 1
    n_line = n_col // 2
    my_parity = my_col % 2
    my_z = my_col // 2
    width = terms.shape[-1]

    def half(array, index):
        rows = array.shape[0] // 2
        return lax.dynamic_slice_in_dim(array, index * rows, rows, 0)

    def row_bit(step):
        place = jnp.where(my_parity == 0, step, bits - 1 - step)
        return (my_row >> place) & 1

    part = terms.reshape(-1, width)
    part = half(part, my_parity) + lax.ppermute(half(part, 1 - my_parity), "col", core_swap(n_col))
    for step in range(bits):
        bit = row_bit(step)
        part = half(part, bit) + lax.ppermute(half(part, 1 - bit), AXES, row_swap(n_row, n_col, step))
    rows = part.shape[0] // n_line

    def line_piece(shift):
        return lax.dynamic_slice_in_dim(part, (my_z + shift) % n_line * rows, rows, 0)

    total = line_piece(0)
    for shift in range(1, n_line):
        total = total + lax.ppermute(line_piece(n_line - shift), "col", line_shift(n_col, shift))
    got = [total] + [lax.ppermute(total, "col", line_shift(n_col, shift)) for shift in range(1, n_line)]
    stacked = jnp.concatenate(got + got, axis=0)
    whole = lax.dynamic_slice_in_dim(stacked, (n_line - my_z) % n_line * rows, n_line * rows, 0)
    for step in reversed(range(bits)):
        other = lax.ppermute(whole, AXES, row_swap(n_row, n_col, step))
        bit = row_bit(step)
        whole = jnp.where(bit == 0, jnp.concatenate([whole, other]), jnp.concatenate([other, whole]))
    other = lax.ppermute(whole, "col", core_swap(n_col))
    whole = jnp.where(my_parity == 0, jnp.concatenate([whole, other]), jnp.concatenate([other, whole]))
    return whole.reshape(terms.shape)


def local(inverse, panels, block_slot, list_ids):
    supernodes, own_rows, width = panels.shape
    row_blocks = inverse.shape[0] // BS
    col_blocks = inverse.shape[1] // BS
    listed = list_ids.shape[1]
    n_row = lax.axis_size("row")
    n_col = lax.axis_size("col")
    n_line = n_col // 2
    per_col = listed // n_col
    max_rows = 2 * listed // n_row
    max_cols = -(-col_blocks // GROUP) * GROUP
    sub = BS // n_row
    my_row = lax.axis_index("row")
    my_col = lax.axis_index("col")

    block_ids = jnp.arange(block_slot.shape[0], dtype=jnp.int32)
    slots = jnp.sum(jnp.where(list_ids[..., None] == block_ids, block_slot, 0), axis=-1)
    in_row = slots // row_blocks == my_row
    in_col = slots // col_blocks == my_col
    row_table = pick_table(in_row, slots % row_blocks, max_rows)
    col_table = pick_table(in_col, slots % col_blocks, max_cols)
    scalars = jnp.stack(
        [
            jnp.sum(in_row.astype(jnp.int32), axis=1),
            jnp.sum(in_col.astype(jnp.int32), axis=1),
            jnp.full((supernodes,), my_row, jnp.int32),
            jnp.full((supernodes,), my_col, jnp.int32),
        ],
        axis=1,
    )
    tables = jnp.concatenate(
        [row_table.reshape(supernodes, -1), col_table.reshape(supernodes, -1), scalars], axis=1
    )

    own = panels.reshape(supernodes, per_col, BS, width)
    own_other = lax.ppermute(own, "col", core_swap(n_col))
    dims = (n_row, n_col, per_col, max_rows, max_cols, sub)
    parts = []
    diag_terms = []
    for supernode in range(supernodes):
        mine = lax.dynamic_slice_in_dim(own[supernode], my_row * sub, sub, 1)
        line = jnp.concatenate(
            [lax.ppermute(mine, "col", line_shift(n_col, shift)) for shift in range(1, n_line)], axis=0
        )
        pieces = [line]
        for e in range(1, n_row):
            bit = e.bit_length() - 1
            pieces.append(lax.ppermute(pieces[e ^ (1 << bit)], AXES, row_swap(n_row, n_col, bit)))
        other = [lax.ppermute(piece, "col", core_swap(n_col)) for piece in pieces]
        coded, plain, diag = products(
            tables[supernode], inverse, (own[supernode], own_other[supernode]), (pieces, other), dims
        )
        coded = lax.ppermute(coded, "col", core_swap(n_col))
        first, *rest = pair_sums(plain, coded)
        moved = [
            lax.ppermute(part, "col", line_shift(n_col, n_line - shift)) for shift, part in enumerate(rest, 1)
        ]
        parts.append([first] + moved)
        diag_terms.append(diag)
    total = sum_over_all(jnp.stack(diag_terms), n_row, n_col, my_row, my_col)
    return final_sums(parts), -total


def solution(mesh):
    return jax.shard_map(
        local,
        mesh=mesh,
        in_specs=(P("row", "col"), P(None, "col", None), P(), P()),
        out_specs=(P(None, ("row", "col"), None), P()),
        check_vma=False,
    )
```

```python
import functools

import jax
import jax.numpy as jnp
from jax import lax
from jax.experimental import pallas as pl
from jax.experimental.pallas import tpu as pltpu
from jax.sharding import PartitionSpec as P

BS = 128
GROUP = 4
TAIL = 16
AXES = ("row", "col")


def swap_bit(bits, parity, bit):
    return 1 << (bit if parity == 0 else bits - 1 - bit)


def row_swap(n_row, n_col, bit):
    bits = n_row.bit_length() - 1
    return [
        ((r ^ swap_bit(bits, c % 2, bit)) * n_col + c, r * n_col + c)
        for r in range(n_row)
        for c in range(n_col)
    ]


def core_swap(n_col):
    return [(c ^ 1, c) for c in range(n_col)]


def line_shift(n_col, shift):
    return [((c + 2 * shift) % n_col, c) for c in range(n_col)]


def pick_table(hit, value, capacity):
    listed = hit.shape[1]
    pos = jnp.arange(listed, dtype=jnp.int32)
    ahead = (pos[:, None] < pos[None, :]) & hit[:, :, None]
    rank = jnp.sum(ahead.astype(jnp.int32), axis=1)
    here = hit[:, None, :] & (rank[:, None, :] == jnp.arange(capacity, dtype=jnp.int32)[None, :, None])
    both = jnp.stack([jnp.broadcast_to(pos, hit.shape), value], axis=1)
    return jnp.sum(jnp.where(here[:, None], both[:, :, None, :], 0), axis=-1)


def encode(rows):
    top = jnp.max(jnp.abs(rows), axis=0, keepdims=True)
    exponent = jnp.ceil(jnp.log2(jnp.maximum(top * (1 + 2.0**-12), 2.0**-100)))
    coded = (rows * jnp.exp2(15.0 - exponent) + 32768.5).astype(jnp.int32) - 32768
    tail = jnp.broadcast_to(exponent, (TAIL, rows.shape[1]))
    return coded.astype(jnp.int16), tail.astype(jnp.int32).astype(jnp.int16)


def decode(coded, tail):
    scale = jnp.exp2(tail[0:1].astype(jnp.int32).astype(jnp.float32) - 15.0)
    return coded.astype(jnp.int32).astype(jnp.float32) * scale


def start_fetch(dims, supernode, my_row, my_col, own, pieces, listed, buf, at, sem):
    n_row, n_col, per_col, _, _, sub = dims
    bits = n_row.bit_length() - 1
    n_line = n_col // 2
    source = lax.div(listed, per_col)
    item = lax.rem(listed, per_col)
    parity = lax.rem(source, 2)
    swapped = parity != lax.rem(my_col, 2)
    shift = lax.rem(lax.div(source, 2) - lax.div(my_col, 2) + n_line, n_line)
    start = pl.multiple_of(at * BS, BS)
    for other in (0, 1):
        mine = swapped if other else jnp.logical_not(swapped)

        @pl.when(mine & (shift == 0))
        def _(other=other):
            pltpu.make_async_copy(own[other].at[supernode * per_col + item], buf.at[pl.ds(start, BS)], sem).start()

        @pl.when(mine & (shift != 0))
        def _(other=other):
            for e in range(n_row):
                masks = [sum(swap_bit(bits, p, b) for b in range(bits) if e >> b & 1) for p in (0, 1)]
                mask = jnp.where(parity == 0, masks[0], masks[1])
                place = pl.multiple_of(start + (my_row ^ mask) * sub, sub)
                pltpu.make_async_copy(
                    pieces[other][e].at[(shift - 1) * per_col + item], buf.at[pl.ds(place, sub)], sem
                ).start()


def wait_fetch(buf, at, sem):
    part = buf.at[pl.ds(pl.multiple_of(at * BS, BS), BS)]
    pltpu.make_async_copy(part, part, sem).wait()


def clear_block(buf, at):
    buf[pl.ds(pl.multiple_of(at * BS, BS), BS), :] = jnp.zeros((BS, buf.shape[1]), buf.dtype)


def slot_of(dims, my_col, parity, at):
    _, n_col, _, max_rows, _, _ = dims
    in_chunk = max_rows // n_col
    n_line = n_col // 2
    chunk = 2 * lax.rem(lax.div(my_col, 2) + lax.div(at, in_chunk), n_line) + parity
    return chunk * in_chunk + lax.rem(at, in_chunk)


def pack_kernel(tab, strip, out):
    out[...] = strip[...]


def pack_strips(tab, inverse, dims):
    _, _, _, max_rows, max_cols, _ = dims
    base = 2 * max_rows + 2 * max_cols
    count = max_rows // 2
    block = (BS, inverse.shape[1])

    def strip(at, tab):
        my_col = tab[base + 3]
        return tab[max_rows + slot_of(dims, my_col, 1 - lax.rem(my_col, 2), at)], 0

    return pl.pallas_call(
        pack_kernel,
        out_shape=jax.ShapeDtypeStruct((count * BS, inverse.shape[1]), inverse.dtype),
        grid_spec=pltpu.PrefetchScalarGridSpec(
            num_scalar_prefetch=1,
            grid=(count,),
            in_specs=[pl.BlockSpec(block, strip)],
            out_specs=pl.BlockSpec(block, lambda at, tab: (at, 0)),
        ),
        cost_estimate=pl.CostEstimate(flops=0, bytes_accessed=27 * 10**6, transcendentals=0),
        name="pack_strips",
    )(tab, inverse)


def product_kernel(dims, supernode, tab, inverse, packed, *refs):
    n_row, n_col, _, max_rows, max_cols, _ = dims
    n_line = n_col // 2
    in_chunk = max_rows // n_col
    own = refs[0:2]
    pieces = (refs[2 : 2 + n_row], refs[2 + n_row : 2 + 2 * n_row])
    first_ref, diag, *outs = refs[2 + 2 * n_row : -7]
    total, cols_buf, rows_buf, strips, cols_sem, rows_sem, strip_sem = refs[-7:]
    step = pl.program_id(0)
    chunk_rows = in_chunk * BS
    group_rows = GROUP * BS
    half_cols = inverse.shape[1]
    base = 2 * max_rows + 2 * max_cols
    n_rows, n_cols, my_row, my_col = tab[base], tab[base + 1], tab[base + 2], tab[base + 3]
    my_parity = lax.rem(my_col, 2)
    slots = strips.shape[0]

    def strip_copies(at, item, slot):
        block = tab[max_rows + slot_of(dims, my_col, my_parity, at * in_chunk + item)]
        rows = pl.ds(item * BS, BS)
        sem = strip_sem.at[slot, item]
        return (
            pltpu.make_async_copy(
                inverse.at[pl.ds(pl.multiple_of(block * BS, BS), BS)], strips.at[slot, rows, pl.ds(0, half_cols)], sem.at[0]
            ),
            pltpu.make_async_copy(
                packed.at[pl.ds(pl.multiple_of((at * in_chunk + item) * BS, BS), BS)],
                strips.at[slot, rows, pl.ds(half_cols, half_cols)],
                sem.at[1],
            ),
        )

    def left_of(at):
        return n_rows - slot_of(dims, my_col, my_parity, at * in_chunk)

    def start_strips(at, slot):
        @pl.when(left_of(at) > 0)
        def _():
            for item in range(in_chunk):
                for copy in strip_copies(at, item, slot):
                    copy.start()

    slot = lax.rem(step, slots)

    @pl.when(step == 0)
    def _():
        start_strips(0, 0)

        @pl.loop(0, n_cols)
        def _(j):
            listed = tab[2 * max_rows + j]
            start_fetch(dims, supernode, my_row, my_col, own, pieces, listed, cols_buf, j, cols_sem.at[j])

        for ahead in range(1, slots - 1):
            start_strips(ahead, ahead)

        @pl.loop(0, n_line * in_chunk)
        def _(at):
            k = slot_of(dims, my_col, my_parity, at)

            @pl.when(k < n_rows)
            def _():
                start_fetch(dims, supernode, my_row, my_col, own, pieces, tab[k], rows_buf, at, rows_sem.at[at])

            @pl.when(k >= n_rows)
            def _():
                clear_block(rows_buf, at)

        @pl.loop(n_cols, lax.div(n_cols + GROUP - 1, GROUP) * GROUP)
        def _(j):
            clear_block(cols_buf, j)

        diag[...] = jnp.zeros_like(diag)

        @pl.loop(0, n_cols)
        def _(j):
            wait_fetch(cols_buf, j, cols_sem.at[j])

    @pl.when(step + slots - 1 < n_line)
    def _():
        start_strips(step + slots - 1, lax.rem(step + slots - 1, slots))

    left = left_of(step)

    @pl.when((left <= 0) | (n_cols == 0))
    def _():
        total[...] = jnp.zeros_like(total)

    @pl.when(left > 0)
    def _():
        for item in range(in_chunk):
            for copy in strip_copies(step, item, slot):
                copy.wait()

        def term(k):
            parts = []
            for item in range(GROUP):
                col = tab[2 * max_rows + max_cols + k * GROUP + item]
                parts.append(strips[slot, :, pl.ds(pl.multiple_of(col * BS, BS), BS)])
            right = cols_buf[pl.ds(pl.multiple_of(k * group_rows, group_rows), group_rows), :]
            return jnp.dot(jnp.concatenate(parts, axis=1), right, preferred_element_type=jnp.float32)

        @pl.when(n_cols > 0)
        def _():
            total[...] = term(0)

        @pl.loop(1, lax.div(n_cols + GROUP - 1, GROUP))
        def _(k):
            total[...] += term(k)

        for item in range(in_chunk):

            @pl.when(item >= left)
            def _(item=item):
                total[pl.ds(item * BS, BS), :] = jnp.zeros((BS, total.shape[1]), total.dtype)

            @pl.when(item < left)
            def _(item=item):
                wait_fetch(rows_buf, step * in_chunk + item, rows_sem.at[step * in_chunk + item])

        sums = total[...]
        high = sums.astype(jnp.bfloat16)
        low = (sums - high.astype(jnp.float32)).astype(jnp.bfloat16)
        rows = rows_buf[pl.ds(pl.multiple_of(step * chunk_rows, chunk_rows), chunk_rows), :].T
        rows = jnp.concatenate([rows, rows], axis=1)
        both = jnp.concatenate([high, low], axis=0)
        diag[...] -= jnp.dot(rows, both, preferred_element_type=jnp.float32)

    @pl.when(step == 0)
    def _():
        first_ref[...] = total[...]

    for shift, out in enumerate(outs, 1):

        @pl.when(step == shift)
        def _(out=out):
            body, tail = encode(total[...])
            out[0:chunk_rows, :] = body
            out[chunk_rows:, :] = tail


def products(tab, inverse, packed, own, pieces, dims, supernode):
    _, n_col, _, max_rows, max_cols, _ = dims
    n_line = n_col // 2
    width = own[0].shape[-1]
    in_chunk = max_rows // n_col
    chunk_rows = in_chunk * BS
    coded_shape = (chunk_rows + TAIL, width)
    any_spec = pl.BlockSpec(memory_space=pl.ANY)
    whole = lambda shape: pl.BlockSpec(shape, lambda g, tab: (0, 0))
    operands = [inverse, packed, *own, *pieces[0], *pieces[1]]
    return pl.pallas_call(
        functools.partial(product_kernel, dims, supernode),
        out_shape=(
            jax.ShapeDtypeStruct((chunk_rows, width), jnp.float32),
            jax.ShapeDtypeStruct((width, width), jnp.float32),
        )
        + (jax.ShapeDtypeStruct(coded_shape, jnp.int16),) * (n_line - 1),
        grid_spec=pltpu.PrefetchScalarGridSpec(
            num_scalar_prefetch=1,
            grid=(n_line,),
            in_specs=[any_spec] * len(operands),
            out_specs=[whole((chunk_rows, width)), whole((width, width))] + [whole(coded_shape)] * (n_line - 1),
            scratch_shapes=[
                pltpu.VMEM((chunk_rows, width), jnp.float32),
                pltpu.VMEM((max_cols * BS, width), jnp.bfloat16),
                pltpu.VMEM((n_line * chunk_rows, width), jnp.bfloat16),
                pltpu.VMEM((3, chunk_rows, 2 * inverse.shape[1]), jnp.bfloat16),
                pltpu.SemaphoreType.DMA((max_cols,)),
                pltpu.SemaphoreType.DMA((n_line * in_chunk,)),
                pltpu.SemaphoreType.DMA((3, in_chunk, 2)),
            ],
        ),
        cost_estimate=pl.CostEstimate(flops=10**10, bytes_accessed=3 * 10**7, transcendentals=0),
        name="products",
    )(tab, *operands)


def final_kernel(count, first, *refs):
    out = refs[-1]
    total = first[...]
    for part in range(count):
        total = total + decode(refs[part][...], refs[count + part][...])
    out[0] = total


def final_sums(supernodes, supernode, first, coded, earlier):
    chunk_rows, width = first.shape
    rows = chunk_rows // 2
    tile = lambda: pl.BlockSpec((rows, width), lambda g: (g, 0))
    tail = lambda: pl.BlockSpec((TAIL, width), lambda g: (chunk_rows // TAIL, 0))
    operands = [first, *coded, *coded]
    specs = [tile()] + [tile()] * len(coded) + [tail()] * len(coded)
    aliases = {}
    if earlier is not None:
        aliases = {len(operands): 0}
        operands.append(earlier)
        specs.append(pl.BlockSpec(memory_space=pl.ANY))
    return pl.pallas_call(
        functools.partial(final_kernel, len(coded)),
        out_shape=jax.ShapeDtypeStruct((supernodes, chunk_rows, width), jnp.float32),
        grid=(2,),
        in_specs=specs,
        out_specs=pl.BlockSpec((1, rows, width), lambda g: (supernode, g, 0)),
        input_output_aliases=aliases,
        cost_estimate=pl.CostEstimate(flops=10**7, bytes_accessed=4 * 10**6, transcendentals=0),
        name="final_sums",
    )(*operands)


def half(array, index):
    rows = array.shape[0] // 2
    return lax.dynamic_slice_in_dim(array, index * rows, rows, 0)


def row_bit(bits, step, my_row, my_parity):
    place = jnp.where(my_parity == 0, step, bits - 1 - step)
    return (my_row >> place) & 1


def sum_over_all(part, n_row, n_col, my_row, my_parity):
    bits = n_row.bit_length() - 1
    n_line = n_col // 2
    part = half(part, my_parity) + lax.ppermute(half(part, 1 - my_parity), "col", core_swap(n_col))
    for step in range(bits):
        bit = row_bit(bits, step, my_row, my_parity)
        part = half(part, bit) + lax.ppermute(half(part, 1 - bit), AXES, row_swap(n_row, n_col, step))
    got = [lax.ppermute(part, "col", line_shift(n_col, shift)) for shift in range(1, n_line)]
    whole = sum(got, part)
    for step in reversed(range(bits)):
        other = lax.ppermute(whole, AXES, row_swap(n_row, n_col, step))
        bit = row_bit(bits, step, my_row, my_parity)
        whole = jnp.where(bit == 0, jnp.concatenate([whole, other]), jnp.concatenate([other, whole]))
    return whole, lax.ppermute(whole, "col", core_swap(n_col))


def local(inverse, panels, block_slot, list_ids):
    supernodes, _, width = panels.shape
    row_blocks = inverse.shape[0] // BS
    col_blocks = inverse.shape[1] // BS
    listed = list_ids.shape[1]
    n_row = lax.axis_size("row")
    n_col = lax.axis_size("col")
    n_line = n_col // 2
    per_col = listed // n_col
    max_rows = 2 * listed // n_row
    max_cols = max_rows if n_col == 2 * n_row else -(-2 * col_blocks // GROUP) * GROUP
    sub = BS // n_row
    my_row = lax.axis_index("row")
    my_col = lax.axis_index("col")

    block_ids = jnp.arange(block_slot.shape[0], dtype=jnp.int32)
    slots = jnp.sum(jnp.where(list_ids[..., None] == block_ids, block_slot, 0), axis=-1)
    in_row = slots // row_blocks == my_row
    in_col = slots // (2 * col_blocks) == my_col // 2
    place = (slots // col_blocks != my_col).astype(jnp.int32) * col_blocks + slots % col_blocks
    row_table = pick_table(in_row, slots % row_blocks, max_rows)
    col_table = pick_table(in_col, place, max_cols)
    scalars = jnp.stack(
        [
            jnp.sum(in_row.astype(jnp.int32), axis=1),
            jnp.sum(in_col.astype(jnp.int32), axis=1),
            jnp.full((supernodes,), my_row, jnp.int32),
            jnp.full((supernodes,), my_col, jnp.int32),
        ],
        axis=1,
    )
    tables = jnp.concatenate(
        [row_table.reshape(supernodes, -1), col_table.reshape(supernodes, -1), scalars], axis=1
    )

    blocks = panels.reshape(supernodes * per_col, BS, width)
    own = (blocks, lax.ppermute(blocks, "col", core_swap(n_col)))
    dims = (n_row, n_col, per_col, max_rows, max_cols, sub)
    held = []
    for s in range(supernodes):
        mine = lax.dynamic_slice(
            blocks, (s * per_col, my_row * sub, 0), (per_col, sub, width)
        )
        line = jnp.concatenate(
            [lax.ppermute(mine, "col", line_shift(n_col, shift)) for shift in range(1, n_line)], axis=0
        )
        pieces = [line]
        for e in range(1, n_row):
            bit = e.bit_length() - 1
            pieces.append(lax.ppermute(pieces[e ^ (1 << bit)], AXES, row_swap(n_row, n_col, bit)))
        other = [lax.ppermute(piece, "col", core_swap(n_col)) for piece in pieces]
        held.append((pieces, other))
    out = None
    halves = []
    for s in range(supernodes):
        packed = pack_strips(tables[s], inverse, dims)
        packed = lax.ppermute(packed, "col", core_swap(n_col))
        first, diag, *coded = products(tables[s], inverse, packed, own, held[s], dims, s)
        coded = [lax.ppermute(part, "col", line_shift(n_col, n_line - shift)) for shift, part in enumerate(coded, 1)]
        halves.append(sum_over_all(diag, n_row, n_col, my_row, my_col % 2))
        out = final_sums(supernodes, s, first, coded, out)
    even = jnp.concatenate([part for mine, other in halves for part in (mine, other)])
    odd = jnp.concatenate([part for mine, other in halves for part in (other, mine)])
    return out, jnp.where(my_col % 2 == 0, even, odd).reshape(supernodes, width, width)


def solution(mesh):
    return jax.shard_map(
        local,
        mesh=mesh,
        in_specs=(P("row", "col"), P(None, "col", None), P(), P()),
        out_specs=(P(None, ("row", "col"), None), P()),
        check_vma=False,
    )
```

```python
import functools

import jax
import jax.numpy as jnp
from jax import lax
from jax.experimental import pallas as pl
from jax.experimental.pallas import tpu as pltpu
from jax.sharding import PartitionSpec as P

BS = 128
GROUP = 4
TAIL = 16
AXES = ("row", "col")


def swap_bit(bits, parity, bit):
    return 1 << (bit if parity == 0 else bits - 1 - bit)


def row_swap(n_row, n_col, bit):
    bits = n_row.bit_length() - 1
    return [
        ((r ^ swap_bit(bits, c % 2, bit)) * n_col + c, r * n_col + c)
        for r in range(n_row)
        for c in range(n_col)
    ]


def row_jump(n_row, n_col, directions):
    bits = n_row.bit_length() - 1
    masks = [sum(swap_bit(bits, p, b) for b in range(bits) if directions >> b & 1) for p in (0, 1)]
    return [((r ^ masks[c % 2]) * n_col + c, r * n_col + c) for r in range(n_row) for c in range(n_col)]


def core_swap(n_col):
    return [(c ^ 1, c) for c in range(n_col)]


def line_swap(n_col, mask):
    return [(c ^ (2 * mask), c) for c in range(n_col)]


def inward(n_col):
    return [(c, c + 2 if c < 2 else c - 2) for c in range(n_col) if c < 2 or c >= n_col - 2]


def across(n_col):
    return [(c, (c ^ 6)) for c in range(2, n_col - 2)]


def line_shift(n_col, shift):
    return [((c + 2 * shift) % n_col, c) for c in range(n_col)]


def pick_table(hit, value, capacity):
    listed = hit.shape[1]
    pos = jnp.arange(listed, dtype=jnp.int32)
    ahead = (pos[:, None] < pos[None, :]) & hit[:, :, None]
    rank = jnp.sum(ahead.astype(jnp.int32), axis=1)
    here = hit[:, None, :] & (rank[:, None, :] == jnp.arange(capacity, dtype=jnp.int32)[None, :, None])
    both = jnp.stack([jnp.broadcast_to(pos, hit.shape), value], axis=1)
    return jnp.sum(jnp.where(here[:, None], both[:, :, None, :], 0), axis=-1)


def encode(rows):
    top = jnp.max(jnp.abs(rows), axis=0, keepdims=True)
    exponent = jnp.ceil(jnp.log2(jnp.maximum(top * (1 + 2.0**-12), 2.0**-100)))
    coded = (rows * jnp.exp2(15.0 - exponent) + 32768.5).astype(jnp.int32) - 32768
    tail = jnp.broadcast_to(exponent, (TAIL, rows.shape[1]))
    return coded.astype(jnp.int16), tail.astype(jnp.int32).astype(jnp.int16)


def decode(coded, tail):
    scale = jnp.exp2(tail[0:1].astype(jnp.int32).astype(jnp.float32) - 15.0)
    return coded.astype(jnp.int32).astype(jnp.float32) * scale


def start_fetch(dims, supernode, my_row, my_col, own, pieces, listed, buf, at, sem):
    n_row, n_col, per_col, _, _, sub = dims
    bits = n_row.bit_length() - 1
    n_line = n_col // 2
    source = lax.div(listed, per_col)
    item = lax.rem(listed, per_col)
    parity = lax.rem(source, 2)
    swapped = parity != lax.rem(my_col, 2)
    shift = lax.rem(lax.div(source, 2) - lax.div(my_col, 2) + n_line, n_line)
    start = pl.multiple_of(at * BS, BS)
    for other in (0, 1):
        mine = swapped if other else jnp.logical_not(swapped)

        @pl.when(mine & (shift == 0))
        def _(other=other):
            pltpu.make_async_copy(own[other].at[supernode * per_col + item], buf.at[pl.ds(start, BS)], sem).start()

        @pl.when(mine & (shift != 0))
        def _(other=other):
            for e in range(n_row):
                masks = [sum(swap_bit(bits, p, b) for b in range(bits) if e >> b & 1) for p in (0, 1)]
                mask = jnp.where(parity == 0, masks[0], masks[1])
                place = pl.multiple_of(start + (my_row ^ mask) * sub, sub)
                pltpu.make_async_copy(
                    pieces[other][e].at[(shift - 1) * per_col + item], buf.at[pl.ds(place, sub)], sem
                ).start()


def wait_fetch(buf, at, sem):
    part = buf.at[pl.ds(pl.multiple_of(at * BS, BS), BS)]
    pltpu.make_async_copy(part, part, sem).wait()


def clear_block(buf, at):
    buf[pl.ds(pl.multiple_of(at * BS, BS), BS), :] = jnp.zeros((BS, buf.shape[1]), buf.dtype)


def slot_of(dims, my_col, parity, at):
    _, n_col, _, max_rows, _, _ = dims
    in_chunk = max_rows // n_col
    chunk = 2 * (lax.div(my_col, 2) ^ lax.div(at, in_chunk)) + parity
    return chunk * in_chunk + lax.rem(at, in_chunk)


def pack_kernel(dims, tab, inverse, packed, strips, in_sem, out_sem):
    _, _, _, max_rows, max_cols, _ = dims
    base = 2 * max_rows + 2 * max_cols
    n_rows, my_col = tab[base], tab[base + 3]
    count, depth = max_rows // 2, strips.shape[0]

    def position(at):
        return slot_of(dims, my_col, 1 - lax.rem(my_col, 2), at)

    def copy_in(at):
        block = tab[max_rows + position(at)]
        rows = inverse.at[pl.ds(pl.multiple_of(block * BS, BS), BS)]
        return pltpu.make_async_copy(rows, strips.at[at % depth], in_sem.at[at % depth])

    def copy_out(at):
        return pltpu.make_async_copy(strips.at[at % depth], packed.at[pl.ds(at * BS, BS)], out_sem.at[at % depth])

    def if_listed(at, act):
        @pl.when(position(at) < n_rows)
        def _():
            act()

    ahead = depth // 2
    for at in range(count + depth):
        if at < count:
            if at >= depth:
                if_listed(at - depth, copy_out(at - depth).wait)
            if_listed(at, copy_in(at).start)
        elif at - depth < count:
            if_listed(at - depth, copy_out(at - depth).wait)
        if 0 <= at - ahead < count:
            if_listed(at - ahead, copy_in(at - ahead).wait)
            if_listed(at - ahead, copy_out(at - ahead).start)


def pack_strips(tab, inverse, dims):
    max_rows = dims[3]
    width = inverse.shape[1]
    any_spec = pl.BlockSpec(memory_space=pl.ANY)
    depth = min(8, max_rows // 2)
    return pl.pallas_call(
        functools.partial(pack_kernel, dims),
        out_shape=jax.ShapeDtypeStruct((max_rows // 2 * BS, width), inverse.dtype),
        grid_spec=pltpu.PrefetchScalarGridSpec(
            num_scalar_prefetch=1,
            grid=(1,),
            in_specs=[any_spec],
            out_specs=any_spec,
            scratch_shapes=[
                pltpu.VMEM((depth, BS, width), inverse.dtype),
                pltpu.SemaphoreType.DMA((depth,)),
                pltpu.SemaphoreType.DMA((depth,)),
            ],
        ),
        cost_estimate=pl.CostEstimate(flops=0, bytes_accessed=27 * 10**6, transcendentals=0),
        name="pack_strips",
    )(tab, inverse)


def product_kernel(dims, supernode, tab, inverse, packed, *refs):
    n_row, n_col, _, max_rows, max_cols, _ = dims
    n_line = n_col // 2
    in_chunk = max_rows // n_col
    own = refs[0:2]
    pieces = (refs[2 : 2 + n_row], refs[2 + n_row : 2 + 2 * n_row])
    total_ref, *outs = refs[2 + 2 * n_row : -4]
    cols_buf, strips, cols_sem, strip_sem = refs[-4:]
    total = total_ref.at[0]
    step = pl.program_id(0)
    chunk_rows = in_chunk * BS
    group_rows = GROUP * BS
    half_cols = inverse.shape[1]
    base = 2 * max_rows + 2 * max_cols
    n_rows, n_cols, my_row, my_col = tab[base], tab[base + 1], tab[base + 2], tab[base + 3]
    my_parity = lax.rem(my_col, 2)
    slots = strips.shape[0]

    def strip_copies(at, item, slot):
        block = tab[max_rows + slot_of(dims, my_col, my_parity, at * in_chunk + item)]
        rows = pl.ds(item * BS, BS)
        sem = strip_sem.at[slot, item]
        return (
            pltpu.make_async_copy(
                inverse.at[pl.ds(pl.multiple_of(block * BS, BS), BS)], strips.at[slot, rows, pl.ds(0, half_cols)], sem.at[0]
            ),
            pltpu.make_async_copy(
                packed.at[pl.ds(pl.multiple_of((at * in_chunk + item) * BS, BS), BS)],
                strips.at[slot, rows, pl.ds(half_cols, half_cols)],
                sem.at[1],
            ),
        )

    def left_of(at):
        return n_rows - slot_of(dims, my_col, my_parity, at * in_chunk)

    def start_strips(at, slot):
        @pl.when(left_of(at) > 0)
        def _():
            for item in range(in_chunk):
                for copy in strip_copies(at, item, slot):
                    copy.start()

    slot = lax.rem(step, slots)

    @pl.when(step == 0)
    def _():
        start_strips(0, 0)

        @pl.loop(0, n_cols)
        def _(j):
            listed = tab[2 * max_rows + j]
            start_fetch(dims, supernode, my_row, my_col, own, pieces, listed, cols_buf, j, cols_sem.at[j])

        for ahead in range(1, slots - 1):
            start_strips(ahead, ahead)

        @pl.loop(n_cols, lax.div(n_cols + GROUP - 1, GROUP) * GROUP)
        def _(j):
            clear_block(cols_buf, j)

        @pl.loop(0, n_cols)
        def _(j):
            wait_fetch(cols_buf, j, cols_sem.at[j])

    @pl.when(step + slots - 1 < n_line)
    def _():
        start_strips(step + slots - 1, lax.rem(step + slots - 1, slots))

    left = left_of(step)

    @pl.when((left <= 0) | (n_cols == 0))
    def _():
        total[...] = jnp.zeros_like(total)

    @pl.when(left > 0)
    def _():
        for item in range(in_chunk):
            for copy in strip_copies(step, item, slot):
                copy.wait()

        def term(k):
            parts = []
            for item in range(GROUP):
                col = tab[2 * max_rows + max_cols + k * GROUP + item]
                parts.append(strips[slot, :, pl.ds(pl.multiple_of(col * BS, BS), BS)])
            right = cols_buf[pl.ds(pl.multiple_of(k * group_rows, group_rows), group_rows), :]
            return jnp.dot(jnp.concatenate(parts, axis=1), right, preferred_element_type=jnp.float32)

        @pl.when(n_cols > 0)
        def _():
            total[...] = term(0)

        @pl.loop(1, lax.div(n_cols + GROUP - 1, GROUP))
        def _(k):
            total[...] += term(k)

        for item in range(in_chunk):

            @pl.when(item >= left)
            def _(item=item):
                total[pl.ds(item * BS, BS), :] = jnp.zeros((BS, total.shape[1]), total.dtype)


    for mask, out in zip(coded_masks(n_line), outs):

        @pl.when(step == mask)
        def _(out=out):
            body, tail = encode(total[...])
            out[0:chunk_rows, :] = body
            out[chunk_rows:, :] = tail


def coded_masks(n_line):
    return (1, 3) if n_line == 4 else tuple(range(1, n_line))


def products(tab, inverse, packed, own, pieces, dims, supernode):
    _, n_col, _, max_rows, max_cols, _ = dims
    n_line = n_col // 2
    width = own[0].shape[-1]
    in_chunk = max_rows // n_col
    chunk_rows = in_chunk * BS
    coded_shape = (chunk_rows + TAIL, width)
    any_spec = pl.BlockSpec(memory_space=pl.ANY)
    whole = lambda shape: pl.BlockSpec(shape, lambda g, tab: (0, 0))
    operands = [inverse, packed, *own, *pieces[0], *pieces[1]]
    return pl.pallas_call(
        functools.partial(product_kernel, dims, supernode),
        out_shape=(jax.ShapeDtypeStruct((n_line, chunk_rows, width), jnp.float32),)
        + (jax.ShapeDtypeStruct(coded_shape, jnp.int16),) * len(coded_masks(n_line)),
        grid_spec=pltpu.PrefetchScalarGridSpec(
            num_scalar_prefetch=1,
            grid=(n_line,),
            in_specs=[any_spec] * len(operands),
            out_specs=[pl.BlockSpec((1, chunk_rows, width), lambda g, tab: (g, 0, 0))]
            + [whole(coded_shape)] * len(coded_masks(n_line)),
            scratch_shapes=[
                pltpu.VMEM((max_cols * BS, width), jnp.bfloat16),
                pltpu.VMEM((3, chunk_rows, 2 * inverse.shape[1]), jnp.bfloat16),
                pltpu.SemaphoreType.DMA((max_cols,)),
                pltpu.SemaphoreType.DMA((3, in_chunk, 2)),
            ],
        ),
        cost_estimate=pl.CostEstimate(flops=10**10, bytes_accessed=3 * 10**7, transcendentals=0),
        name="products",
    )(tab, *operands)


def diag_kernel(dims, supernode, tab, total, *refs):
    n_row, n_col, _, max_rows, max_cols, _ = dims
    n_line = n_col // 2
    in_chunk = max_rows // n_col
    own = refs[0:2]
    pieces = (refs[2 : 2 + n_row], refs[2 + n_row : 2 + 2 * n_row])
    sent, kept, diag, rows_buf, rows_sem = refs[2 + 2 * n_row :]
    step = pl.program_id(0)
    chunk_rows = in_chunk * BS
    base = 2 * max_rows + 2 * max_cols
    n_rows, my_row, my_col = tab[base], tab[base + 2], tab[base + 3]
    my_parity = lax.rem(my_col, 2)

    @pl.when(step == 0)
    def _():
        @pl.loop(0, n_line * in_chunk)
        def _(at):
            k = slot_of(dims, my_col, my_parity, at)

            @pl.when(k < n_rows)
            def _():
                start_fetch(dims, supernode, my_row, my_col, own, pieces, tab[k], rows_buf, at, rows_sem.at[at])

            @pl.when(k >= n_rows)
            def _():
                clear_block(rows_buf, at)

        diag[...] = jnp.zeros_like(diag)

    left = n_rows - slot_of(dims, my_col, my_parity, step * in_chunk)

    @pl.when(left > 0)
    def _():
        for item in range(in_chunk):

            @pl.when(item < left)
            def _(item=item):
                wait_fetch(rows_buf, step * in_chunk + item, rows_sem.at[step * in_chunk + item])

        sums = total[0]
        high = sums.astype(jnp.bfloat16)
        low = (sums - high.astype(jnp.float32)).astype(jnp.bfloat16)
        rows = rows_buf[pl.ds(pl.multiple_of(step * chunk_rows, chunk_rows), chunk_rows), :].T
        rows = jnp.concatenate([rows, rows], axis=1)
        both = jnp.concatenate([high, low], axis=0)
        diag[...] -= jnp.dot(rows, both, preferred_element_type=jnp.float32)

    @pl.when(step == n_line - 1)
    def _():
        rows = sent.shape[0]
        sent[...] = diag[pl.ds(pl.multiple_of((1 - my_parity) * rows, rows), rows), :]
        kept[...] = diag[pl.ds(pl.multiple_of(my_parity * rows, rows), rows), :]


def diag_terms(tab, total, own, pieces, dims, supernode):
    n_line, chunk_rows, width = total.shape
    any_spec = pl.BlockSpec(memory_space=pl.ANY)
    operands = [*own, *pieces[0], *pieces[1]]
    return pl.pallas_call(
        functools.partial(diag_kernel, dims, supernode),
        out_shape=(jax.ShapeDtypeStruct((width // 2, width), jnp.float32),) * 2,
        grid_spec=pltpu.PrefetchScalarGridSpec(
            num_scalar_prefetch=1,
            grid=(n_line,),
            in_specs=[pl.BlockSpec((1, chunk_rows, width), lambda g, tab: (g, 0, 0))] + [any_spec] * len(operands),
            out_specs=[pl.BlockSpec((width // 2, width), lambda g, tab: (0, 0))] * 2,
            scratch_shapes=[
                pltpu.VMEM((width, width), jnp.float32),
                pltpu.VMEM((n_line * chunk_rows, width), jnp.bfloat16),
                pltpu.SemaphoreType.DMA((n_line * chunk_rows // BS,)),
            ],
        ),
        cost_estimate=pl.CostEstimate(flops=3 * 10**9, bytes_accessed=7 * 10**6, transcendentals=0),
        name="diag_terms",
    )(tab, total, *operands)


def join_kernel(total, far, out):
    rows = total.shape[1]
    body, tail = encode(total[0] + decode(far[0:rows, :], far[rows:, :]))
    out[0:rows, :] = body
    out[rows:, :] = tail


def join_far(total, far):
    _, chunk_rows, width = total.shape
    coded = pl.BlockSpec(far.shape, lambda g: (0, 0))
    return pl.pallas_call(
        join_kernel,
        out_shape=jax.ShapeDtypeStruct(far.shape, far.dtype),
        grid=(1,),
        in_specs=[pl.BlockSpec((1, chunk_rows, width), lambda g: (2, 0, 0)), coded],
        out_specs=coded,
        cost_estimate=pl.CostEstimate(flops=10**7, bytes_accessed=2 * 10**6, transcendentals=0),
        name="join_far",
    )(total, far)


def final_kernel(count, first, *refs):
    out = refs[-1]
    total = first[0]
    for part in range(count):
        total = total + decode(refs[part][...], refs[count + part][...])
    out[0] = total


def final_sums(supernodes, supernode, first, coded, earlier):
    _, chunk_rows, width = first.shape
    rows = chunk_rows // 2
    tile = lambda: pl.BlockSpec((rows, width), lambda g: (g, 0))
    tail = lambda: pl.BlockSpec((TAIL, width), lambda g: (chunk_rows // TAIL, 0))
    operands = [first, *coded, *coded]
    specs = [pl.BlockSpec((1, rows, width), lambda g: (0, g, 0))] + [tile()] * len(coded) + [tail()] * len(coded)
    aliases = {}
    if earlier is not None:
        aliases = {len(operands): 0}
        operands.append(earlier)
        specs.append(pl.BlockSpec(memory_space=pl.ANY))
    return pl.pallas_call(
        functools.partial(final_kernel, len(coded)),
        out_shape=jax.ShapeDtypeStruct((supernodes, chunk_rows, width), jnp.float32),
        grid=(2,),
        in_specs=specs,
        out_specs=pl.BlockSpec((1, rows, width), lambda g: (supernode, g, 0)),
        input_output_aliases=aliases,
        cost_estimate=pl.CostEstimate(flops=10**7, bytes_accessed=4 * 10**6, transcendentals=0),
        name="final_sums",
    )(*operands)


def half(array, index):
    rows = array.shape[0] // 2
    return lax.dynamic_slice_in_dim(array, index * rows, rows, 0)


def row_bit(bits, step, my_row, my_parity):
    place = jnp.where(my_parity == 0, step, bits - 1 - step)
    return (my_row >> place) & 1


def sum_over_all(sent, kept, n_row, n_col, my_row, my_parity):
    bits = n_row.bit_length() - 1
    n_line = n_col // 2
    got = lax.ppermute(sent, "col", core_swap(n_col))
    for step in range(bits):
        bit = row_bit(bits, step, my_row, my_parity)
        sent = half(kept, 1 - bit) + half(got, 1 - bit)
        kept = half(kept, bit) + half(got, bit)
        got = lax.ppermute(sent, AXES, row_swap(n_row, n_col, step))
    part = kept + got
    got = [lax.ppermute(part, "col", line_shift(n_col, shift)) for shift in range(1, n_line)]
    whole = sum(got, part)
    for step in reversed(range(bits)):
        other = lax.ppermute(whole, AXES, row_swap(n_row, n_col, step))
        bit = row_bit(bits, step, my_row, my_parity)
        whole = jnp.where(bit == 0, jnp.concatenate([whole, other]), jnp.concatenate([other, whole]))
    return whole, lax.ppermute(whole, "col", core_swap(n_col))


def place_kernel(parity, mine, other, *refs):
    out = refs[-1]

    @pl.when(pl.program_id(0) == parity[0])
    def _():
        out[0] = mine[...]

    @pl.when(pl.program_id(0) != parity[0])
    def _():
        out[0] = other[...]


def place_halves(supernodes, supernode, parity, mine, other, earlier):
    rows, width = mine.shape
    whole = pl.BlockSpec((rows, width), lambda g, parity: (0, 0))
    operands, specs, aliases = [mine, other], [whole, whole], {}
    if earlier is not None:
        aliases = {3: 0}
        operands.append(earlier)
        specs.append(pl.BlockSpec(memory_space=pl.ANY))
    return pl.pallas_call(
        place_kernel,
        out_shape=jax.ShapeDtypeStruct((supernodes, 2 * rows, width), jnp.float32),
        grid_spec=pltpu.PrefetchScalarGridSpec(
            num_scalar_prefetch=1,
            grid=(2,),
            in_specs=specs,
            out_specs=pl.BlockSpec((1, rows, width), lambda g, parity: (supernode, g, 0)),
        ),
        input_output_aliases=aliases,
        cost_estimate=pl.CostEstimate(flops=0, bytes_accessed=2 * 10**6, transcendentals=0),
        name="place_halves",
    )(parity, *operands)


def local(inverse, panels, block_slot, list_ids):
    supernodes, _, width = panels.shape
    row_blocks = inverse.shape[0] // BS
    col_blocks = inverse.shape[1] // BS
    listed = list_ids.shape[1]
    n_row = lax.axis_size("row")
    n_col = lax.axis_size("col")
    n_line = n_col // 2
    per_col = listed // n_col
    max_rows = 2 * listed // n_row
    max_cols = max_rows if n_col == 2 * n_row else -(-2 * col_blocks // GROUP) * GROUP
    sub = BS // n_row
    my_row = lax.axis_index("row")
    my_col = lax.axis_index("col")

    block_ids = jnp.arange(block_slot.shape[0], dtype=jnp.int32)
    slots = jnp.sum(jnp.where(list_ids[..., None] == block_ids, block_slot, 0), axis=-1)
    in_row = slots // row_blocks == my_row
    in_col = slots // (2 * col_blocks) == my_col // 2
    place = (slots // col_blocks != my_col).astype(jnp.int32) * col_blocks + slots % col_blocks
    row_table = pick_table(in_row, slots % row_blocks, max_rows)
    col_table = pick_table(in_col, place, max_cols)
    scalars = jnp.stack(
        [
            jnp.sum(in_row.astype(jnp.int32), axis=1),
            jnp.sum(in_col.astype(jnp.int32), axis=1),
            jnp.full((supernodes,), my_row, jnp.int32),
            jnp.full((supernodes,), my_col, jnp.int32),
        ],
        axis=1,
    )
    tables = jnp.concatenate(
        [row_table.reshape(supernodes, -1), col_table.reshape(supernodes, -1), scalars], axis=1
    )

    blocks = panels.reshape(supernodes * per_col, BS, width)
    own = (blocks, lax.ppermute(blocks, "col", core_swap(n_col)))
    dims = (n_row, n_col, per_col, max_rows, max_cols, sub)
    held = []
    for s in range(supernodes):
        mine = lax.dynamic_slice(
            blocks, (s * per_col, my_row * sub, 0), (per_col, sub, width)
        )
        line = jnp.concatenate(
            [lax.ppermute(mine, "col", line_shift(n_col, shift)) for shift in range(1, n_line)], axis=0
        )
        pieces = [line]
        for e in range(1, n_row):
            bit = e.bit_length() - 1
            if s == 0:
                source, pairs = pieces[e ^ (1 << bit)], row_swap(n_row, n_col, bit)
            else:
                source, pairs = line, row_jump(n_row, n_col, e)
            pieces.append(lax.ppermute(source, AXES, pairs))
        other = [lax.ppermute(piece, "col", core_swap(n_col)) for piece in pieces]
        held.append((pieces, other))
    out = None
    diag = None
    for s in range(supernodes):
        packed = pack_strips(tables[s], inverse, dims)
        packed = lax.ppermute(packed, "col", core_swap(n_col))
        total, *coded = products(tables[s], inverse, packed, own, held[s], dims, s)
        coded = dict(zip(coded_masks(n_line), coded))
        if n_line == 4:
            far = lax.ppermute(coded[3], "col", inward(n_col))
            moved = [lax.ppermute(coded[3], "col", across(n_col)), lax.ppermute(coded[1], "col", line_swap(n_col, 1))]
            joined = join_far(total, far)
            moved.append(lax.ppermute(joined, "col", line_swap(n_col, 2)))
        else:
            moved = [lax.ppermute(part, "col", line_swap(n_col, mask)) for mask, part in coded.items()]
        sent, kept = diag_terms(tables[s], total, own, held[s], dims, s)
        mine, other = sum_over_all(sent, kept, n_row, n_col, my_row, my_col % 2)
        diag = place_halves(supernodes, s, (my_col % 2).reshape(1), mine, other, diag)
        out = final_sums(supernodes, s, total, moved, out)
    return out, diag


def solution(mesh):
    return jax.shard_map(
        local,
        mesh=mesh,
        in_specs=(P("row", "col"), P(None, "col", None), P(), P()),
        out_specs=(P(None, ("row", "col"), None), P()),
        check_vma=False,
    )
```

```python
import functools

import jax
import jax.numpy as jnp
from jax import lax
from jax.experimental import pallas as pl
from jax.experimental.pallas import tpu as pltpu
from jax.sharding import PartitionSpec as P

BS = 128
GROUP = 8
TAIL = 16
AXES = ("row", "col")


def swap_bit(bits, parity, bit):
    return 1 << (bit if parity == 0 else bits - 1 - bit)


def row_swap(n_row, n_col, bit):
    bits = n_row.bit_length() - 1
    return [
        ((r ^ swap_bit(bits, c % 2, bit)) * n_col + c, r * n_col + c)
        for r in range(n_row)
        for c in range(n_col)
    ]


def row_jump(n_row, n_col, directions):
    bits = n_row.bit_length() - 1
    masks = [sum(swap_bit(bits, p, b) for b in range(bits) if directions >> b & 1) for p in (0, 1)]
    return [((r ^ masks[c % 2]) * n_col + c, r * n_col + c) for r in range(n_row) for c in range(n_col)]


def core_swap(n_col):
    return [(c ^ 1, c) for c in range(n_col)]


def line_swap(n_col, mask):
    return [(c ^ (2 * mask), c) for c in range(n_col)]


def inward(n_col):
    return [(c, c + 2 if c < 2 else c - 2) for c in range(n_col) if c < 2 or c >= n_col - 2]


def across(n_col):
    return [(c, (c ^ 6)) for c in range(2, n_col - 2)]


def line_shift(n_col, shift):
    return [((c + 2 * shift) % n_col, c) for c in range(n_col)]


def pick_table(hit, value, capacity):
    listed = hit.shape[1]
    pos = jnp.arange(listed, dtype=jnp.int32)
    ahead = (pos[:, None] < pos[None, :]) & hit[:, :, None]
    rank = jnp.sum(ahead.astype(jnp.int32), axis=1)
    here = hit[:, None, :] & (rank[:, None, :] == jnp.arange(capacity, dtype=jnp.int32)[None, :, None])
    both = jnp.stack([jnp.broadcast_to(pos, hit.shape), value], axis=1)
    return jnp.sum(jnp.where(here[:, None], both[:, :, None, :], 0), axis=-1)


def encode(rows):
    top = jnp.max(jnp.abs(rows), axis=0, keepdims=True)
    exponent = jnp.ceil(jnp.log2(jnp.maximum(top * (1 + 2.0**-12), 2.0**-100)))
    coded = (rows * jnp.exp2(15.0 - exponent) + 32768.5).astype(jnp.int32) - 32768
    tail = jnp.broadcast_to(exponent, (TAIL, rows.shape[1]))
    return coded.astype(jnp.int16), tail.astype(jnp.int32).astype(jnp.int16)


def decode(coded, tail):
    scale = jnp.exp2(tail[0:1].astype(jnp.int32).astype(jnp.float32) - 15.0)
    return coded.astype(jnp.int32).astype(jnp.float32) * scale


def start_fetch(dims, supernode, my_row, my_col, own, pieces, listed, buf, at, sem):
    n_row, n_col, per_col, _, _, sub = dims
    bits = n_row.bit_length() - 1
    n_line = n_col // 2
    source = lax.div(listed, per_col)
    item = lax.rem(listed, per_col)
    parity = lax.rem(source, 2)
    swapped = parity != lax.rem(my_col, 2)
    shift = lax.rem(lax.div(source, 2) - lax.div(my_col, 2) + n_line, n_line)
    start = pl.multiple_of(at * BS, BS)
    for other in (0, 1):
        mine = swapped if other else jnp.logical_not(swapped)

        @pl.when(mine & (shift == 0))
        def _(other=other):
            pltpu.make_async_copy(own[other].at[supernode * per_col + item], buf.at[pl.ds(start, BS)], sem).start()

        span = (n_line - 1) // len(pieces)
        for part, sides in enumerate(pieces):
            here = mine & (shift > part * span) & (shift <= (part + 1) * span)

            @pl.when(here)
            def _(side=sides[other], before=part * span + 1):
                for e in range(n_row):
                    masks = [sum(swap_bit(bits, p, b) for b in range(bits) if e >> b & 1) for p in (0, 1)]
                    mask = jnp.where(parity == 0, masks[0], masks[1])
                    place = pl.multiple_of(start + (my_row ^ mask) * sub, sub)
                    source_ref = side[e].at[(shift - before) * per_col + item]
                    pltpu.make_async_copy(source_ref, buf.at[pl.ds(place, sub)], sem).start()


def panel_refs(refs, n_row, parts):
    sides = [refs[2 + n_row * at : 2 + n_row * (at + 1)] for at in range(2 * parts)]
    return refs[0:2], [sides[2 * part : 2 * part + 2] for part in range(parts)], refs[2 + 2 * n_row * parts :]


def wait_fetch(buf, at, sem):
    part = buf.at[pl.ds(pl.multiple_of(at * BS, BS), BS)]
    pltpu.make_async_copy(part, part, sem).wait()


def clear_block(buf, at):
    buf[pl.ds(pl.multiple_of(at * BS, BS), BS), :] = jnp.zeros((BS, buf.shape[1]), buf.dtype)


def slot_of(dims, my_col, parity, at):
    _, n_col, _, max_rows, _, _ = dims
    in_chunk = max_rows // n_col
    chunk = 2 * (lax.div(my_col, 2) ^ lax.div(at, in_chunk)) + parity
    return chunk * in_chunk + lax.rem(at, in_chunk)


def pack_kernel(dims, tab, inverse, packed, strips, in_sem, out_sem):
    _, _, _, max_rows, max_cols, _ = dims
    base = 2 * max_rows + 2 * max_cols
    n_rows, my_col = tab[base], tab[base + 3]
    count, depth = max_rows // 2, strips.shape[0]

    def position(at):
        return slot_of(dims, my_col, 1 - lax.rem(my_col, 2), at)

    def copy_in(at):
        block = tab[max_rows + position(at)]
        rows = inverse.at[pl.ds(pl.multiple_of(block * BS, BS), BS)]
        return pltpu.make_async_copy(rows, strips.at[at % depth], in_sem.at[at % depth])

    def copy_out(at):
        return pltpu.make_async_copy(strips.at[at % depth], packed.at[pl.ds(at * BS, BS)], out_sem.at[at % depth])

    def if_listed(at, act):
        @pl.when(position(at) < n_rows)
        def _():
            act()

    ahead = depth // 2
    for at in range(count + depth):
        if at < count:
            if at >= depth:
                if_listed(at - depth, copy_out(at - depth).wait)
            if_listed(at, copy_in(at).start)
        elif at - depth < count:
            if_listed(at - depth, copy_out(at - depth).wait)
        if 0 <= at - ahead < count:
            if_listed(at - ahead, copy_in(at - ahead).wait)
            if_listed(at - ahead, copy_out(at - ahead).start)


def pack_strips(tab, inverse, dims):
    max_rows = dims[3]
    width = inverse.shape[1]
    any_spec = pl.BlockSpec(memory_space=pl.ANY)
    depth = min(8, max_rows // 2)
    return pl.pallas_call(
        functools.partial(pack_kernel, dims),
        out_shape=jax.ShapeDtypeStruct((max_rows // 2 * BS, width), inverse.dtype),
        grid_spec=pltpu.PrefetchScalarGridSpec(
            num_scalar_prefetch=1,
            grid=(1,),
            in_specs=[any_spec],
            out_specs=any_spec,
            scratch_shapes=[
                pltpu.VMEM((depth, BS, width), inverse.dtype),
                pltpu.SemaphoreType.DMA((depth,)),
                pltpu.SemaphoreType.DMA((depth,)),
            ],
        ),
        cost_estimate=pl.CostEstimate(flops=0, bytes_accessed=27 * 10**6, transcendentals=0),
        name="pack_strips",
    )(tab, inverse)


def product_kernel(dims, supernode, parts, tab, inverse, packed, *refs):
    n_row, n_col, _, max_rows, max_cols, _ = dims
    n_line = n_col // 2
    in_chunk = max_rows // n_col
    own, pieces, refs = panel_refs(refs, n_row, parts)
    total_ref, *outs = refs[:-4]
    cols_buf, strips, cols_sem, strip_sem = refs[-4:]
    total = total_ref.at[0]
    step = pl.program_id(0)
    chunk_rows = in_chunk * BS
    group_rows = GROUP * BS
    half_cols = inverse.shape[1]
    base = 2 * max_rows + 2 * max_cols
    n_rows, n_cols, my_row, my_col = tab[base], tab[base + 1], tab[base + 2], tab[base + 3]
    my_parity = lax.rem(my_col, 2)
    slots = strips.shape[0]

    def strip_copies(at, item, slot):
        block = tab[max_rows + slot_of(dims, my_col, my_parity, at * in_chunk + item)]
        rows = pl.ds(item * BS, BS)
        sem = strip_sem.at[slot, item]
        return (
            pltpu.make_async_copy(
                inverse.at[pl.ds(pl.multiple_of(block * BS, BS), BS)], strips.at[slot, rows, pl.ds(0, half_cols)], sem.at[0]
            ),
            pltpu.make_async_copy(
                packed.at[pl.ds(pl.multiple_of((at * in_chunk + item) * BS, BS), BS)],
                strips.at[slot, rows, pl.ds(half_cols, half_cols)],
                sem.at[1],
            ),
        )

    def left_of(at):
        return n_rows - slot_of(dims, my_col, my_parity, at * in_chunk)

    def start_strips(at, slot):
        @pl.when(left_of(at) > 0)
        def _():
            for item in range(in_chunk):
                for copy in strip_copies(at, item, slot):
                    copy.start()

    slot = lax.rem(step, slots)

    @pl.when(step == 0)
    def _():
        start_strips(0, 0)

        @pl.loop(0, n_cols)
        def _(j):
            listed = tab[2 * max_rows + j]
            start_fetch(dims, supernode, my_row, my_col, own, pieces, listed, cols_buf, j, cols_sem.at[j])

        for ahead in range(1, slots - 1):
            start_strips(ahead, ahead)

        @pl.loop(n_cols, lax.div(n_cols + GROUP - 1, GROUP) * GROUP)
        def _(j):
            clear_block(cols_buf, j)

        @pl.loop(0, n_cols)
        def _(j):
            wait_fetch(cols_buf, j, cols_sem.at[j])

    @pl.when(step + slots - 1 < n_line)
    def _():
        start_strips(step + slots - 1, lax.rem(step + slots - 1, slots))

    left = left_of(step)

    @pl.when((left <= 0) | (n_cols == 0))
    def _():
        total[...] = jnp.zeros_like(total)

    @pl.when(left > 0)
    def _():
        for item in range(in_chunk):
            for copy in strip_copies(step, item, slot):
                copy.wait()

        def term(k):
            parts = []
            for item in range(GROUP):
                col = tab[2 * max_rows + max_cols + k * GROUP + item]
                parts.append(strips[slot, :, pl.ds(pl.multiple_of(col * BS, BS), BS)])
            right = cols_buf[pl.ds(pl.multiple_of(k * group_rows, group_rows), group_rows), :]
            return jnp.dot(jnp.concatenate(parts, axis=1), right, preferred_element_type=jnp.float32)

        @pl.when(n_cols > 0)
        def _():
            total[...] = term(0)

        @pl.loop(1, lax.div(n_cols + GROUP - 1, GROUP))
        def _(k):
            total[...] += term(k)

        for item in range(in_chunk):

            @pl.when(item >= left)
            def _(item=item):
                total[pl.ds(item * BS, BS), :] = jnp.zeros((BS, total.shape[1]), total.dtype)


    for mask, out in zip(coded_masks(n_line), outs):

        @pl.when(step == mask)
        def _(out=out):
            body, tail = encode(total[...])
            out[0:chunk_rows, :] = body
            out[chunk_rows:, :] = tail


def coded_masks(n_line):
    return (1, 3) if n_line == 4 else tuple(range(1, n_line))


def products(tab, inverse, packed, own, pieces, dims, supernode):
    _, n_col, _, max_rows, max_cols, _ = dims
    n_line = n_col // 2
    width = own[0].shape[-1]
    in_chunk = max_rows // n_col
    chunk_rows = in_chunk * BS
    coded_shape = (chunk_rows + TAIL, width)
    any_spec = pl.BlockSpec(memory_space=pl.ANY)
    whole = lambda shape: pl.BlockSpec(shape, lambda g, tab: (0, 0))
    operands = [inverse, packed, *own, *(piece for sides in pieces for side in sides for piece in side)]
    return pl.pallas_call(
        functools.partial(product_kernel, dims, supernode, len(pieces)),
        out_shape=(jax.ShapeDtypeStruct((n_line, chunk_rows, width), jnp.float32),)
        + (jax.ShapeDtypeStruct(coded_shape, jnp.int16),) * len(coded_masks(n_line)),
        grid_spec=pltpu.PrefetchScalarGridSpec(
            num_scalar_prefetch=1,
            grid=(n_line,),
            in_specs=[any_spec] * len(operands),
            out_specs=[pl.BlockSpec((1, chunk_rows, width), lambda g, tab: (g, 0, 0))]
            + [whole(coded_shape)] * len(coded_masks(n_line)),
            scratch_shapes=[
                pltpu.VMEM((max_cols * BS, width), jnp.bfloat16),
                pltpu.VMEM((3, chunk_rows, 2 * inverse.shape[1]), jnp.bfloat16),
                pltpu.SemaphoreType.DMA((max_cols,)),
                pltpu.SemaphoreType.DMA((3, in_chunk, 2)),
            ],
        ),
        cost_estimate=pl.CostEstimate(flops=10**10, bytes_accessed=3 * 10**7, transcendentals=0),
        name="products",
    )(tab, *operands)


def diag_kernel(dims, supernode, parts, tab, total, *refs):
    n_row, n_col, _, max_rows, max_cols, _ = dims
    n_line = n_col // 2
    in_chunk = max_rows // n_col
    own, pieces, refs = panel_refs(refs, n_row, parts)
    sent, kept, diag, rows_buf, rows_sem = refs
    step = pl.program_id(0)
    chunk_rows = in_chunk * BS
    base = 2 * max_rows + 2 * max_cols
    n_rows, my_row, my_col = tab[base], tab[base + 2], tab[base + 3]
    my_parity = lax.rem(my_col, 2)

    @pl.when(step == 0)
    def _():
        @pl.loop(0, n_line * in_chunk)
        def _(at):
            k = slot_of(dims, my_col, my_parity, at)

            @pl.when(k < n_rows)
            def _():
                start_fetch(dims, supernode, my_row, my_col, own, pieces, tab[k], rows_buf, at, rows_sem.at[at])

            @pl.when(k >= n_rows)
            def _():
                clear_block(rows_buf, at)

        diag[...] = jnp.zeros_like(diag)

    left = n_rows - slot_of(dims, my_col, my_parity, step * in_chunk)

    @pl.when(left > 0)
    def _():
        for item in range(in_chunk):

            @pl.when(item < left)
            def _(item=item):
                wait_fetch(rows_buf, step * in_chunk + item, rows_sem.at[step * in_chunk + item])

        sums = total[0]
        high = sums.astype(jnp.bfloat16)
        low = (sums - high.astype(jnp.float32)).astype(jnp.bfloat16)
        rows = rows_buf[pl.ds(pl.multiple_of(step * chunk_rows, chunk_rows), chunk_rows), :].T
        rows = jnp.concatenate([rows, rows], axis=1)
        both = jnp.concatenate([high, low], axis=0)
        diag[...] -= jnp.dot(rows, both, preferred_element_type=jnp.float32)

    @pl.when(step == n_line - 1)
    def _():
        rows = sent.shape[0]
        sent[...] = diag[pl.ds(pl.multiple_of((1 - my_parity) * rows, rows), rows), :]
        kept[...] = diag[pl.ds(pl.multiple_of(my_parity * rows, rows), rows), :]


def diag_terms(tab, total, own, pieces, dims, supernode):
    n_line, chunk_rows, width = total.shape
    any_spec = pl.BlockSpec(memory_space=pl.ANY)
    operands = [*own, *(piece for sides in pieces for side in sides for piece in side)]
    return pl.pallas_call(
        functools.partial(diag_kernel, dims, supernode, len(pieces)),
        out_shape=(jax.ShapeDtypeStruct((width // 2, width), jnp.float32),) * 2,
        grid_spec=pltpu.PrefetchScalarGridSpec(
            num_scalar_prefetch=1,
            grid=(n_line,),
            in_specs=[pl.BlockSpec((1, chunk_rows, width), lambda g, tab: (g, 0, 0))] + [any_spec] * len(operands),
            out_specs=[pl.BlockSpec((width // 2, width), lambda g, tab: (0, 0))] * 2,
            scratch_shapes=[
                pltpu.VMEM((width, width), jnp.float32),
                pltpu.VMEM((n_line * chunk_rows, width), jnp.bfloat16),
                pltpu.SemaphoreType.DMA((n_line * chunk_rows // BS,)),
            ],
        ),
        cost_estimate=pl.CostEstimate(flops=3 * 10**9, bytes_accessed=7 * 10**6, transcendentals=0),
        name="diag_terms",
    )(tab, total, *operands)


def join_kernel(total, far, out):
    rows = total.shape[1]
    body, tail = encode(total[0] + decode(far[0:rows, :], far[rows:, :]))
    out[0:rows, :] = body
    out[rows:, :] = tail


def join_far(total, far):
    _, chunk_rows, width = total.shape
    coded = pl.BlockSpec(far.shape, lambda g: (0, 0))
    return pl.pallas_call(
        join_kernel,
        out_shape=jax.ShapeDtypeStruct(far.shape, far.dtype),
        grid=(1,),
        in_specs=[pl.BlockSpec((1, chunk_rows, width), lambda g: (2, 0, 0)), coded],
        out_specs=coded,
        cost_estimate=pl.CostEstimate(flops=10**7, bytes_accessed=2 * 10**6, transcendentals=0),
        name="join_far",
    )(total, far)


def final_kernel(count, first, *refs):
    out = refs[-1]
    total = first[0]
    for part in range(count):
        total = total + decode(refs[part][...], refs[count + part][...])
    out[0] = total


def final_sums(supernodes, supernode, first, coded, earlier):
    _, chunk_rows, width = first.shape
    rows = chunk_rows // 2
    tile = lambda: pl.BlockSpec((rows, width), lambda g: (g, 0))
    tail = lambda: pl.BlockSpec((TAIL, width), lambda g: (chunk_rows // TAIL, 0))
    operands = [first, *coded, *coded]
    specs = [pl.BlockSpec((1, rows, width), lambda g: (0, g, 0))] + [tile()] * len(coded) + [tail()] * len(coded)
    aliases = {}
    if earlier is not None:
        aliases = {len(operands): 0}
        operands.append(earlier)
        specs.append(pl.BlockSpec(memory_space=pl.ANY))
    return pl.pallas_call(
        functools.partial(final_kernel, len(coded)),
        out_shape=jax.ShapeDtypeStruct((supernodes, chunk_rows, width), jnp.float32),
        grid=(2,),
        in_specs=specs,
        out_specs=pl.BlockSpec((1, rows, width), lambda g: (supernode, g, 0)),
        input_output_aliases=aliases,
        cost_estimate=pl.CostEstimate(flops=10**7, bytes_accessed=4 * 10**6, transcendentals=0),
        name="final_sums",
    )(*operands)


def half(array, index):
    rows = array.shape[0] // 2
    return lax.dynamic_slice_in_dim(array, index * rows, rows, 0)


def row_bit(bits, step, my_row, my_parity):
    place = jnp.where(my_parity == 0, step, bits - 1 - step)
    return (my_row >> place) & 1


def halve_sum(sent, kept, n_row, n_col, my_row, my_parity):
    bits = n_row.bit_length() - 1
    got = lax.ppermute(sent, "col", core_swap(n_col))
    for step in range(bits):
        bit = row_bit(bits, step, my_row, my_parity)
        sent = half(kept, 1 - bit) + half(got, 1 - bit)
        kept = half(kept, bit) + half(got, bit)
        got = lax.ppermute(sent, AXES, row_swap(n_row, n_col, step))
    return kept, got


def fold_kernel(*refs):
    total, coded = refs[-2:]
    supernodes, rows, _ = total.shape
    for s in range(supernodes):
        total[s] = refs[2 * s][...] + refs[2 * s + 1][...]
    body, tail = encode(total[...].reshape(supernodes * rows, total.shape[2]))
    coded[0 : supernodes * rows, :] = body
    coded[supernodes * rows :, :] = tail


def fold_pieces(terms):
    rows, width = terms[0].shape
    supernodes = len(terms) // 2
    return pl.pallas_call(
        fold_kernel,
        out_shape=(
            jax.ShapeDtypeStruct((supernodes, rows, width), jnp.float32),
            jax.ShapeDtypeStruct((supernodes * rows + TAIL, width), jnp.int16),
        ),
        cost_estimate=pl.CostEstimate(flops=10**6, bytes_accessed=10**6, transcendentals=0),
        name="fold_pieces",
    )(*terms)


def line_kernel(total, *refs):
    out = refs[-1]
    supernodes, rows, _ = out.shape
    for s in range(supernodes):
        piece = total[s]
        for part in refs[:-1]:
            piece = piece + decode(part[s * rows : (s + 1) * rows, :], part[supernodes * rows :, :])
        out[s] = piece


def line_sums(total, coded):
    return pl.pallas_call(
        line_kernel,
        out_shape=jax.ShapeDtypeStruct(total.shape, jnp.float32),
        cost_estimate=pl.CostEstimate(flops=10**6, bytes_accessed=10**6, transcendentals=0),
        name="line_sums",
    )(total, *coded)


def place_kernel(parity, mine, other, out):
    @pl.when(pl.program_id(1) == parity[0])
    def _():
        out[...] = mine[...]

    @pl.when(pl.program_id(1) != parity[0])
    def _():
        out[...] = other[...]


def place_halves(parity, mine, other):
    supernodes, rows, width = mine.shape
    block = pl.BlockSpec((1, rows, width), lambda s, g, parity: (s, 0, 0))
    return pl.pallas_call(
        place_kernel,
        out_shape=jax.ShapeDtypeStruct((supernodes, 2 * rows, width), jnp.float32),
        grid_spec=pltpu.PrefetchScalarGridSpec(
            num_scalar_prefetch=1,
            grid=(supernodes, 2),
            in_specs=[block, block],
            out_specs=pl.BlockSpec((1, rows, width), lambda s, g, parity: (s, g, 0)),
        ),
        cost_estimate=pl.CostEstimate(flops=0, bytes_accessed=4 * 10**6, transcendentals=0),
        name="place_halves",
    )(parity, mine, other)


def local(inverse, panels, block_slot, list_ids):
    supernodes, _, width = panels.shape
    row_blocks = inverse.shape[0] // BS
    col_blocks = inverse.shape[1] // BS
    listed = list_ids.shape[1]
    n_row = lax.axis_size("row")
    n_col = lax.axis_size("col")
    n_line = n_col // 2
    per_col = listed // n_col
    max_rows = 2 * listed // n_row
    max_cols = max_rows if n_col == 2 * n_row else -(-2 * col_blocks // GROUP) * GROUP
    sub = BS // n_row
    my_row = lax.axis_index("row")
    my_col = lax.axis_index("col")

    block_ids = jnp.arange(block_slot.shape[0], dtype=jnp.int32)
    slots = jnp.sum(jnp.where(list_ids[..., None] == block_ids, block_slot, 0), axis=-1)
    in_row = slots // row_blocks == my_row
    in_col = slots // (2 * col_blocks) == my_col // 2
    place = (slots // col_blocks != my_col).astype(jnp.int32) * col_blocks + slots % col_blocks
    row_table = pick_table(in_row, slots % row_blocks, max_rows)
    col_table = pick_table(in_col, place, max_cols)
    scalars = jnp.stack(
        [
            jnp.sum(in_row.astype(jnp.int32), axis=1),
            jnp.sum(in_col.astype(jnp.int32), axis=1),
            jnp.full((supernodes,), my_row, jnp.int32),
            jnp.full((supernodes,), my_col, jnp.int32),
        ],
        axis=1,
    )
    tables = jnp.concatenate(
        [row_table.reshape(supernodes, -1), col_table.reshape(supernodes, -1), scalars], axis=1
    )

    blocks = panels.reshape(supernodes * per_col, BS, width)
    own = (blocks, lax.ppermute(blocks, "col", core_swap(n_col)))
    dims = (n_row, n_col, per_col, max_rows, max_cols, sub)
    held = []
    for s in range(supernodes):
        mine = lax.dynamic_slice(blocks, (s * per_col, my_row * sub, 0), (per_col, sub, width))
        got = [lax.ppermute(mine, "col", line_shift(n_col, shift)) for shift in range(1, n_line)]
        if s > 0 or n_line > 4:
            got = [jnp.concatenate(got, axis=0)]
        held.append([])
        for line in got:
            pieces = [line]
            for e in range(1, n_row):
                bit = e.bit_length() - 1
                if s == 0:
                    source, pairs = pieces[e ^ (1 << bit)], row_swap(n_row, n_col, bit)
                else:
                    source, pairs = line, row_jump(n_row, n_col, e)
                pieces.append(lax.ppermute(source, AXES, pairs))
            other = [lax.ppermute(piece, "col", core_swap(n_col)) for piece in pieces]
            held[s].append((pieces, other))
    out = None
    terms = []
    for s in range(supernodes):
        packed = pack_strips(tables[s], inverse, dims)
        packed = lax.ppermute(packed, "col", core_swap(n_col))
        total, *coded = products(tables[s], inverse, packed, own, held[s], dims, s)
        coded = dict(zip(coded_masks(n_line), coded))
        if n_line == 4:
            far = lax.ppermute(coded[3], "col", inward(n_col))
            moved = [lax.ppermute(coded[3], "col", across(n_col)), lax.ppermute(coded[1], "col", line_swap(n_col, 1))]
            joined = join_far(total, far)
            moved.append(lax.ppermute(joined, "col", line_swap(n_col, 2)))
        else:
            moved = [lax.ppermute(part, "col", line_swap(n_col, mask)) for mask, part in coded.items()]
        sent, kept = diag_terms(tables[s], total, own, held[s], dims, s)
        terms += halve_sum(sent, kept, n_row, n_col, my_row, my_col % 2)
        out = final_sums(supernodes, s, total, moved, out)
    bits = n_row.bit_length() - 1
    total, coded = fold_pieces(terms)
    coded = [lax.ppermute(coded, "col", line_shift(n_col, shift)) for shift in range(1, n_line)]
    whole = line_sums(total, coded)
    for step in reversed(range(bits)):
        other = lax.ppermute(whole, AXES, row_swap(n_row, n_col, step))
        low = row_bit(bits, step, my_row, my_col % 2) == 0
        whole = jnp.where(
            low, jnp.concatenate([whole, other], axis=1), jnp.concatenate([other, whole], axis=1)
        )
    other = lax.ppermute(whole, "col", core_swap(n_col))
    return out, place_halves((my_col % 2).reshape(1), whole, other)


def solution(mesh):
    return jax.shard_map(
        local,
        mesh=mesh,
        in_specs=(P("row", "col"), P(None, "col", None), P(), P()),
        out_specs=(P(None, ("row", "col"), None), P()),
        check_vma=False,
    )
```

```python
import functools

import jax
import jax.numpy as jnp
from jax import lax
from jax.experimental import pallas as pl
from jax.experimental.pallas import tpu as pltpu
from jax.sharding import PartitionSpec as P

BS = 128
GROUP = 16
TAIL = 16
AXES = ("row", "col")


def swap_bit(bits, parity, bit):
    return 1 << (bit if parity == 0 else bits - 1 - bit)


def row_swap(n_row, n_col, bit):
    bits = n_row.bit_length() - 1
    return [
        ((r ^ swap_bit(bits, c % 2, bit)) * n_col + c, r * n_col + c)
        for r in range(n_row)
        for c in range(n_col)
    ]


def row_jump(n_row, n_col, directions):
    bits = n_row.bit_length() - 1
    masks = [sum(swap_bit(bits, p, b) for b in range(bits) if directions >> b & 1) for p in (0, 1)]
    return [((r ^ masks[c % 2]) * n_col + c, r * n_col + c) for r in range(n_row) for c in range(n_col)]


def core_swap(n_col):
    return [(c ^ 1, c) for c in range(n_col)]


def line_swap(n_col, mask):
    return [(c ^ (2 * mask), c) for c in range(n_col)]


def inward(n_col):
    return [(c, c + 2 if c < 2 else c - 2) for c in range(n_col) if c < 2 or c >= n_col - 2]


def across(n_col):
    return [(c, (c ^ 6)) for c in range(2, n_col - 2)]


def line_shift(n_col, shift):
    return [((c + 2 * shift) % n_col, c) for c in range(n_col)]


def pick_table(hit, value, capacity):
    listed = hit.shape[1]
    pos = jnp.arange(listed, dtype=jnp.int32)
    ahead = (pos[:, None] < pos[None, :]) & hit[:, :, None]
    rank = jnp.sum(ahead.astype(jnp.int32), axis=1)
    here = hit[:, None, :] & (rank[:, None, :] == jnp.arange(capacity, dtype=jnp.int32)[None, :, None])
    both = jnp.stack([jnp.broadcast_to(pos, hit.shape), value], axis=1)
    return jnp.sum(jnp.where(here[:, None], both[:, :, None, :], 0), axis=-1)


def encode(rows):
    top = jnp.max(jnp.abs(rows), axis=0, keepdims=True)
    exponent = jnp.ceil(jnp.log2(jnp.maximum(top * (1 + 2.0**-12), 2.0**-100)))
    coded = (rows * jnp.exp2(15.0 - exponent) + 32768.5).astype(jnp.int32) - 32768
    tail = jnp.broadcast_to(exponent, (TAIL, rows.shape[1]))
    return coded.astype(jnp.int16), tail.astype(jnp.int32).astype(jnp.int16)


def decode(coded, tail):
    scale = jnp.exp2(tail[0:1].astype(jnp.int32).astype(jnp.float32) - 15.0)
    return coded.astype(jnp.int32).astype(jnp.float32) * scale


def start_fetch(dims, supernode, my_row, my_col, own, pieces, listed, buf, at, sem):
    n_row, n_col, per_col, _, _, sub = dims
    bits = n_row.bit_length() - 1
    n_line = n_col // 2
    source = lax.div(listed, per_col)
    item = lax.rem(listed, per_col)
    parity = lax.rem(source, 2)
    swapped = parity != lax.rem(my_col, 2)
    shift = lax.rem(lax.div(source, 2) - lax.div(my_col, 2) + n_line, n_line)
    start = pl.multiple_of(at * BS, BS)
    for other in (0, 1):
        mine = swapped if other else jnp.logical_not(swapped)

        @pl.when(mine & (shift == 0))
        def _(other=other):
            pltpu.make_async_copy(own[other].at[supernode * per_col + item], buf.at[pl.ds(start, BS)], sem).start()

        span = (n_line - 1) // len(pieces)
        for part, sides in enumerate(pieces):
            here = mine & (shift > part * span) & (shift <= (part + 1) * span)

            @pl.when(here)
            def _(side=sides[other], before=part * span + 1):
                for e in range(n_row):
                    masks = [sum(swap_bit(bits, p, b) for b in range(bits) if e >> b & 1) for p in (0, 1)]
                    mask = jnp.where(parity == 0, masks[0], masks[1])
                    place = pl.multiple_of(start + (my_row ^ mask) * sub, sub)
                    source_ref = side[e].at[(shift - before) * per_col + item]
                    pltpu.make_async_copy(source_ref, buf.at[pl.ds(place, sub)], sem).start()


def panel_refs(refs, n_row, parts):
    sides = [refs[2 + n_row * at : 2 + n_row * (at + 1)] for at in range(2 * parts)]
    return refs[0:2], [sides[2 * part : 2 * part + 2] for part in range(parts)], refs[2 + 2 * n_row * parts :]


def wait_fetch(buf, at, sem):
    part = buf.at[pl.ds(pl.multiple_of(at * BS, BS), BS)]
    pltpu.make_async_copy(part, part, sem).wait()


def clear_block(buf, at):
    buf[pl.ds(pl.multiple_of(at * BS, BS), BS), :] = jnp.zeros((BS, buf.shape[1]), buf.dtype)


def slot_of(dims, my_col, parity, at):
    _, n_col, _, max_rows, _, _ = dims
    in_chunk = max_rows // n_col
    chunk = 2 * (lax.div(my_col, 2) ^ lax.div(at, in_chunk)) + parity
    return chunk * in_chunk + lax.rem(at, in_chunk)


def pack_kernel(dims, tab, inverse, packed, strips, in_sem, out_sem):
    _, _, _, max_rows, max_cols, _ = dims
    base = 2 * max_rows + 2 * max_cols
    n_rows, my_col = tab[base], tab[base + 3]
    count, depth = max_rows // 2, strips.shape[0]

    def position(at):
        return slot_of(dims, my_col, 1 - lax.rem(my_col, 2), at)

    def copy_in(at):
        block = tab[max_rows + position(at)]
        rows = inverse.at[pl.ds(pl.multiple_of(block * BS, BS), BS)]
        return pltpu.make_async_copy(rows, strips.at[at % depth], in_sem.at[at % depth])

    def copy_out(at):
        return pltpu.make_async_copy(strips.at[at % depth], packed.at[pl.ds(at * BS, BS)], out_sem.at[at % depth])

    def if_listed(at, act):
        @pl.when(position(at) < n_rows)
        def _():
            act()

    ahead = depth // 2
    for at in range(count + depth):
        if at < count:
            if at >= depth:
                if_listed(at - depth, copy_out(at - depth).wait)
            if_listed(at, copy_in(at).start)
        elif at - depth < count:
            if_listed(at - depth, copy_out(at - depth).wait)
        if 0 <= at - ahead < count:
            if_listed(at - ahead, copy_in(at - ahead).wait)
            if_listed(at - ahead, copy_out(at - ahead).start)


def pack_strips(tab, inverse, dims):
    max_rows = dims[3]
    width = inverse.shape[1]
    any_spec = pl.BlockSpec(memory_space=pl.ANY)
    depth = min(8, max_rows // 2)
    return pl.pallas_call(
        functools.partial(pack_kernel, dims),
        out_shape=jax.ShapeDtypeStruct((max_rows // 2 * BS, width), inverse.dtype),
        grid_spec=pltpu.PrefetchScalarGridSpec(
            num_scalar_prefetch=1,
            grid=(1,),
            in_specs=[any_spec],
            out_specs=any_spec,
            scratch_shapes=[
                pltpu.VMEM((depth, BS, width), inverse.dtype),
                pltpu.SemaphoreType.DMA((depth,)),
                pltpu.SemaphoreType.DMA((depth,)),
            ],
        ),
        cost_estimate=pl.CostEstimate(flops=0, bytes_accessed=27 * 10**6, transcendentals=0),
        name="pack_strips",
    )(tab, inverse)


def product_kernel(dims, supernode, parts, tab, inverse, packed, *refs):
    n_row, n_col, _, max_rows, max_cols, _ = dims
    n_line = n_col // 2
    in_chunk = max_rows // n_col
    own, pieces, refs = panel_refs(refs, n_row, parts)
    total_ref, *outs = refs[:-4]
    cols_buf, strips, cols_sem, strip_sem = refs[-4:]
    total = total_ref.at[0]
    step = pl.program_id(0)
    chunk_rows = in_chunk * BS
    group_rows = GROUP * BS
    half_cols = inverse.shape[1]
    base = 2 * max_rows + 2 * max_cols
    n_rows, n_cols, my_row, my_col = tab[base], tab[base + 1], tab[base + 2], tab[base + 3]
    my_parity = lax.rem(my_col, 2)
    slots = strips.shape[0]

    def strip_copies(at, item, slot):
        block = tab[max_rows + slot_of(dims, my_col, my_parity, at * in_chunk + item)]
        rows = pl.ds(item * BS, BS)
        sem = strip_sem.at[slot, item]
        return (
            pltpu.make_async_copy(
                inverse.at[pl.ds(pl.multiple_of(block * BS, BS), BS)], strips.at[slot, rows, pl.ds(0, half_cols)], sem.at[0]
            ),
            pltpu.make_async_copy(
                packed.at[pl.ds(pl.multiple_of((at * in_chunk + item) * BS, BS), BS)],
                strips.at[slot, rows, pl.ds(half_cols, half_cols)],
                sem.at[1],
            ),
        )

    def left_of(at):
        return n_rows - slot_of(dims, my_col, my_parity, at * in_chunk)

    def start_strips(at, slot):
        @pl.when(left_of(at) > 0)
        def _():
            for item in range(in_chunk):
                for copy in strip_copies(at, item, slot):
                    copy.start()

    slot = lax.rem(step, slots)

    @pl.when(step == 0)
    def _():
        start_strips(0, 0)

        @pl.loop(0, n_cols)
        def _(j):
            listed = tab[2 * max_rows + j]
            start_fetch(dims, supernode, my_row, my_col, own, pieces, listed, cols_buf, j, cols_sem.at[j])

        for ahead in range(1, slots - 1):
            start_strips(ahead, ahead)

        @pl.loop(n_cols, lax.div(n_cols + GROUP - 1, GROUP) * GROUP)
        def _(j):
            clear_block(cols_buf, j)

        @pl.loop(0, n_cols)
        def _(j):
            wait_fetch(cols_buf, j, cols_sem.at[j])

    @pl.when(step + slots - 1 < n_line)
    def _():
        start_strips(step + slots - 1, lax.rem(step + slots - 1, slots))

    left = left_of(step)

    @pl.when((left <= 0) | (n_cols == 0))
    def _():
        total[...] = jnp.zeros_like(total)

    @pl.when(left > 0)
    def _():
        for item in range(in_chunk):
            for copy in strip_copies(step, item, slot):
                copy.wait()

        def term(k):
            parts = []
            for item in range(GROUP):
                col = tab[2 * max_rows + max_cols + k * GROUP + item]
                parts.append(strips[slot, :, pl.ds(pl.multiple_of(col * BS, BS), BS)])
            right = cols_buf[pl.ds(pl.multiple_of(k * group_rows, group_rows), group_rows), :]
            return jnp.dot(jnp.concatenate(parts, axis=1), right, preferred_element_type=jnp.float32)

        @pl.when(n_cols > 0)
        def _():
            total[...] = term(0)

        @pl.loop(1, lax.div(n_cols + GROUP - 1, GROUP))
        def _(k):
            total[...] += term(k)

        for item in range(in_chunk):

            @pl.when(item >= left)
            def _(item=item):
                total[pl.ds(item * BS, BS), :] = jnp.zeros((BS, total.shape[1]), total.dtype)


    for mask, out in zip(coded_masks(n_line), outs):

        @pl.when(step == mask)
        def _(out=out):
            body, tail = encode(total[...])
            out[0:chunk_rows, :] = body
            out[chunk_rows:, :] = tail


def coded_masks(n_line):
    return (1, 3) if n_line == 4 else tuple(range(1, n_line))


def products(tab, inverse, packed, own, pieces, dims, supernode):
    _, n_col, _, max_rows, max_cols, _ = dims
    n_line = n_col // 2
    width = own[0].shape[-1]
    in_chunk = max_rows // n_col
    chunk_rows = in_chunk * BS
    coded_shape = (chunk_rows + TAIL, width)
    any_spec = pl.BlockSpec(memory_space=pl.ANY)
    whole = lambda shape: pl.BlockSpec(shape, lambda g, tab: (0, 0))
    operands = [inverse, packed, *own, *(piece for sides in pieces for side in sides for piece in side)]
    return pl.pallas_call(
        functools.partial(product_kernel, dims, supernode, len(pieces)),
        out_shape=(jax.ShapeDtypeStruct((n_line, chunk_rows, width), jnp.float32),)
        + (jax.ShapeDtypeStruct(coded_shape, jnp.int16),) * len(coded_masks(n_line)),
        grid_spec=pltpu.PrefetchScalarGridSpec(
            num_scalar_prefetch=1,
            grid=(n_line,),
            in_specs=[any_spec] * len(operands),
            out_specs=[pl.BlockSpec((1, chunk_rows, width), lambda g, tab: (g, 0, 0))]
            + [whole(coded_shape)] * len(coded_masks(n_line)),
            scratch_shapes=[
                pltpu.VMEM((max_cols * BS, width), jnp.bfloat16),
                pltpu.VMEM((3, chunk_rows, 2 * inverse.shape[1]), jnp.bfloat16),
                pltpu.SemaphoreType.DMA((max_cols,)),
                pltpu.SemaphoreType.DMA((3, in_chunk, 2)),
            ],
        ),
        cost_estimate=pl.CostEstimate(flops=10**10, bytes_accessed=3 * 10**7, transcendentals=0),
        name="products",
    )(tab, *operands)


def diag_kernel(dims, supernode, parts, tab, total, *refs):
    n_row, n_col, _, max_rows, max_cols, _ = dims
    n_line = n_col // 2
    in_chunk = max_rows // n_col
    own, pieces, refs = panel_refs(refs, n_row, parts)
    sent, kept, diag, rows_buf, rows_sem = refs
    step = pl.program_id(0)
    chunk_rows = in_chunk * BS
    base = 2 * max_rows + 2 * max_cols
    n_rows, my_row, my_col = tab[base], tab[base + 2], tab[base + 3]
    my_parity = lax.rem(my_col, 2)

    @pl.when(step == 0)
    def _():
        @pl.loop(0, n_line * in_chunk)
        def _(at):
            k = slot_of(dims, my_col, my_parity, at)

            @pl.when(k < n_rows)
            def _():
                start_fetch(dims, supernode, my_row, my_col, own, pieces, tab[k], rows_buf, at, rows_sem.at[at])

            @pl.when(k >= n_rows)
            def _():
                clear_block(rows_buf, at)

        diag[...] = jnp.zeros_like(diag)

    left = n_rows - slot_of(dims, my_col, my_parity, step * in_chunk)

    @pl.when(left > 0)
    def _():
        for item in range(in_chunk):

            @pl.when(item < left)
            def _(item=item):
                wait_fetch(rows_buf, step * in_chunk + item, rows_sem.at[step * in_chunk + item])

        sums = total[0]
        high = sums.astype(jnp.bfloat16)
        low = (sums - high.astype(jnp.float32)).astype(jnp.bfloat16)
        rows = rows_buf[pl.ds(pl.multiple_of(step * chunk_rows, chunk_rows), chunk_rows), :].T
        rows = jnp.concatenate([rows, rows], axis=1)
        both = jnp.concatenate([high, low], axis=0)
        diag[...] -= jnp.dot(rows, both, preferred_element_type=jnp.float32)

    @pl.when(step == n_line - 1)
    def _():
        rows = sent.shape[0]
        sent[...] = diag[pl.ds(pl.multiple_of((1 - my_parity) * rows, rows), rows), :]
        kept[...] = diag[pl.ds(pl.multiple_of(my_parity * rows, rows), rows), :]


def diag_terms(tab, total, own, pieces, dims, supernode):
    n_line, chunk_rows, width = total.shape
    any_spec = pl.BlockSpec(memory_space=pl.ANY)
    operands = [*own, *(piece for sides in pieces for side in sides for piece in side)]
    return pl.pallas_call(
        functools.partial(diag_kernel, dims, supernode, len(pieces)),
        out_shape=(jax.ShapeDtypeStruct((width // 2, width), jnp.float32),) * 2,
        grid_spec=pltpu.PrefetchScalarGridSpec(
            num_scalar_prefetch=1,
            grid=(n_line,),
            in_specs=[pl.BlockSpec((1, chunk_rows, width), lambda g, tab: (g, 0, 0))] + [any_spec] * len(operands),
            out_specs=[pl.BlockSpec((width // 2, width), lambda g, tab: (0, 0))] * 2,
            scratch_shapes=[
                pltpu.VMEM((width, width), jnp.float32),
                pltpu.VMEM((n_line * chunk_rows, width), jnp.bfloat16),
                pltpu.SemaphoreType.DMA((n_line * chunk_rows // BS,)),
            ],
        ),
        cost_estimate=pl.CostEstimate(flops=3 * 10**9, bytes_accessed=7 * 10**6, transcendentals=0),
        name="diag_terms",
    )(tab, total, *operands)


def join_kernel(total, far, out):
    rows = total.shape[1]
    body, tail = encode(total[0] + decode(far[0:rows, :], far[rows:, :]))
    out[0:rows, :] = body
    out[rows:, :] = tail


def join_far(total, far):
    _, chunk_rows, width = total.shape
    coded = pl.BlockSpec(far.shape, lambda g: (0, 0))
    return pl.pallas_call(
        join_kernel,
        out_shape=jax.ShapeDtypeStruct(far.shape, far.dtype),
        grid=(1,),
        in_specs=[pl.BlockSpec((1, chunk_rows, width), lambda g: (2, 0, 0)), coded],
        out_specs=coded,
        cost_estimate=pl.CostEstimate(flops=10**7, bytes_accessed=2 * 10**6, transcendentals=0),
        name="join_far",
    )(total, far)


def final_kernel(count, first, *refs):
    out = refs[-1]
    total = first[0]
    for part in range(count):
        total = total + decode(refs[part][...], refs[count + part][...])
    out[0] = total


def final_sums(supernodes, supernode, first, coded, earlier):
    _, chunk_rows, width = first.shape
    rows = chunk_rows // 2
    tile = lambda: pl.BlockSpec((rows, width), lambda g: (g, 0))
    tail = lambda: pl.BlockSpec((TAIL, width), lambda g: (chunk_rows // TAIL, 0))
    operands = [first, *coded, *coded]
    specs = [pl.BlockSpec((1, rows, width), lambda g: (0, g, 0))] + [tile()] * len(coded) + [tail()] * len(coded)
    aliases = {}
    if earlier is not None:
        aliases = {len(operands): 0}
        operands.append(earlier)
        specs.append(pl.BlockSpec(memory_space=pl.ANY))
    return pl.pallas_call(
        functools.partial(final_kernel, len(coded)),
        out_shape=jax.ShapeDtypeStruct((supernodes, chunk_rows, width), jnp.float32),
        grid=(2,),
        in_specs=specs,
        out_specs=pl.BlockSpec((1, rows, width), lambda g: (supernode, g, 0)),
        input_output_aliases=aliases,
        cost_estimate=pl.CostEstimate(flops=10**7, bytes_accessed=4 * 10**6, transcendentals=0),
        name="final_sums",
    )(*operands)


def half(array, index):
    rows = array.shape[0] // 2
    return lax.dynamic_slice_in_dim(array, index * rows, rows, 0)


def row_bit(bits, step, my_row, my_parity):
    place = jnp.where(my_parity == 0, step, bits - 1 - step)
    return (my_row >> place) & 1


def halve_sum(sent, kept, n_row, n_col, my_row, my_parity):
    bits = n_row.bit_length() - 1
    got = lax.ppermute(sent, "col", core_swap(n_col))
    for step in range(bits):
        bit = row_bit(bits, step, my_row, my_parity)
        sent = half(kept, 1 - bit) + half(got, 1 - bit)
        kept = half(kept, bit) + half(got, bit)
        got = lax.ppermute(sent, AXES, row_swap(n_row, n_col, step))
    return kept, got


def fold_kernel(*refs):
    total, coded = refs[-2:]
    supernodes, rows, _ = total.shape
    for s in range(supernodes):
        total[s] = refs[2 * s][...] + refs[2 * s + 1][...]
    body, tail = encode(total[...].reshape(supernodes * rows, total.shape[2]))
    coded[0 : supernodes * rows, :] = body
    coded[supernodes * rows :, :] = tail


def fold_pieces(terms):
    rows, width = terms[0].shape
    supernodes = len(terms) // 2
    return pl.pallas_call(
        fold_kernel,
        out_shape=(
            jax.ShapeDtypeStruct((supernodes, rows, width), jnp.float32),
            jax.ShapeDtypeStruct((supernodes * rows + TAIL, width), jnp.int16),
        ),
        cost_estimate=pl.CostEstimate(flops=10**6, bytes_accessed=10**6, transcendentals=0),
        name="fold_pieces",
    )(*terms)


def line_kernel(total, *refs):
    out = refs[-1]
    supernodes, rows, _ = out.shape
    for s in range(supernodes):
        piece = total[s]
        for part in refs[:-1]:
            piece = piece + decode(part[s * rows : (s + 1) * rows, :], part[supernodes * rows :, :])
        out[s] = piece


def line_sums(total, coded):
    return pl.pallas_call(
        line_kernel,
        out_shape=jax.ShapeDtypeStruct(total.shape, jnp.float32),
        cost_estimate=pl.CostEstimate(flops=10**6, bytes_accessed=10**6, transcendentals=0),
        name="line_sums",
    )(total, *coded)


def place_kernel(at, piece, *refs):
    refs[-1][...] = piece[...]


def place_half(at, piece, earlier):
    supernodes, rows, width = piece.shape
    operands, aliases = [piece], {}
    specs = [pl.BlockSpec(piece.shape, lambda g, at: (0, 0, 0))]
    if earlier is not None:
        aliases = {2: 0}
        operands.append(earlier)
        specs.append(pl.BlockSpec(memory_space=pl.ANY))
    return pl.pallas_call(
        place_kernel,
        out_shape=jax.ShapeDtypeStruct((supernodes, 2 * rows, width), jnp.float32),
        grid_spec=pltpu.PrefetchScalarGridSpec(
            num_scalar_prefetch=1,
            grid=(1,),
            in_specs=specs,
            out_specs=pl.BlockSpec(piece.shape, lambda g, at: (0, at[0], 0)),
        ),
        input_output_aliases=aliases,
        cost_estimate=pl.CostEstimate(flops=0, bytes_accessed=2 * 10**6, transcendentals=0),
        name="place_half",
    )(at, *operands)


def local(inverse, panels, block_slot, list_ids):
    supernodes, _, width = panels.shape
    row_blocks = inverse.shape[0] // BS
    col_blocks = inverse.shape[1] // BS
    listed = list_ids.shape[1]
    n_row = lax.axis_size("row")
    n_col = lax.axis_size("col")
    n_line = n_col // 2
    per_col = listed // n_col
    max_rows = 2 * listed // n_row
    max_cols = max_rows if n_col == 2 * n_row else -(-2 * col_blocks // GROUP) * GROUP
    sub = BS // n_row
    my_row = lax.axis_index("row")
    my_col = lax.axis_index("col")

    block_ids = jnp.arange(block_slot.shape[0], dtype=jnp.int32)
    slots = jnp.sum(jnp.where(list_ids[..., None] == block_ids, block_slot, 0), axis=-1)
    in_row = slots // row_blocks == my_row
    in_col = slots // (2 * col_blocks) == my_col // 2
    place = (slots // col_blocks != my_col).astype(jnp.int32) * col_blocks + slots % col_blocks
    row_table = pick_table(in_row, slots % row_blocks, max_rows)
    col_table = pick_table(in_col, place, max_cols)
    scalars = jnp.stack(
        [
            jnp.sum(in_row.astype(jnp.int32), axis=1),
            jnp.sum(in_col.astype(jnp.int32), axis=1),
            jnp.full((supernodes,), my_row, jnp.int32),
            jnp.full((supernodes,), my_col, jnp.int32),
        ],
        axis=1,
    )
    tables = jnp.concatenate(
        [row_table.reshape(supernodes, -1), col_table.reshape(supernodes, -1), scalars], axis=1
    )

    blocks = panels.reshape(supernodes * per_col, BS, width)
    own = (blocks, lax.ppermute(blocks, "col", core_swap(n_col)))
    dims = (n_row, n_col, per_col, max_rows, max_cols, sub)
    held = []
    for s in range(supernodes):
        mine = lax.dynamic_slice(blocks, (s * per_col, my_row * sub, 0), (per_col, sub, width))
        got = [lax.ppermute(mine, "col", line_shift(n_col, shift)) for shift in range(1, n_line)]
        if s > 0 or n_line > 4:
            got = [jnp.concatenate(got, axis=0)]
        held.append([])
        for line in got:
            pieces = [line]
            for e in range(1, n_row):
                bit = e.bit_length() - 1
                if s == 0:
                    source, pairs = pieces[e ^ (1 << bit)], row_swap(n_row, n_col, bit)
                else:
                    source, pairs = line, row_jump(n_row, n_col, e)
                pieces.append(lax.ppermute(source, AXES, pairs))
            other = [lax.ppermute(piece, "col", core_swap(n_col)) for piece in pieces]
            held[s].append((pieces, other))
    out = None
    terms = []
    for s in range(supernodes):
        packed = pack_strips(tables[s], inverse, dims)
        packed = lax.ppermute(packed, "col", core_swap(n_col))
        total, *coded = products(tables[s], inverse, packed, own, held[s], dims, s)
        coded = dict(zip(coded_masks(n_line), coded))
        if n_line == 4:
            far = lax.ppermute(coded[3], "col", inward(n_col))
            moved = [lax.ppermute(coded[3], "col", across(n_col)), lax.ppermute(coded[1], "col", line_swap(n_col, 1))]
            joined = join_far(total, far)
            moved.append(lax.ppermute(joined, "col", line_swap(n_col, 2)))
        else:
            moved = [lax.ppermute(part, "col", line_swap(n_col, mask)) for mask, part in coded.items()]
        sent, kept = diag_terms(tables[s], total, own, held[s], dims, s)
        terms += halve_sum(sent, kept, n_row, n_col, my_row, my_col % 2)
        out = final_sums(supernodes, s, total, moved, out)
    bits = n_row.bit_length() - 1
    total, coded = fold_pieces(terms)
    coded = [lax.ppermute(coded, "col", line_shift(n_col, shift)) for shift in range(1, n_line)]
    whole = line_sums(total, coded)
    for step in reversed(range(bits)):
        other = lax.ppermute(whole, AXES, row_swap(n_row, n_col, step))
        low = row_bit(bits, step, my_row, my_col % 2) == 0
        whole = jnp.where(
            low, jnp.concatenate([whole, other], axis=1), jnp.concatenate([other, whole], axis=1)
        )
    other = lax.ppermute(whole, "col", core_swap(n_col))
    diag = place_half((my_col % 2).reshape(1), whole, None)
    return out, place_half((1 - my_col % 2).reshape(1), other, diag)


def solution(mesh):
    return jax.shard_map(
        local,
        mesh=mesh,
        in_specs=(P("row", "col"), P(None, "col", None), P(), P()),
        out_specs=(P(None, ("row", "col"), None), P()),
        check_vma=False,
    )
```
